32 devices in a mesh: dp: 2 (over x), row: 4 (over y, core), col: 4 (over z).
Axes of the slice: x: 2, y: 2, z: 4, core: 2. Of those that a mesh axis runs over, the one named last changes fastest.
Arguments:
- block_input: bfloat16 [2048, 1024], P(('dp', 'col'), 'row'), may hold values from -6 to 6
- query_weight: bfloat16 [1024, 2048], P('row', 'col'), may hold values from -0.1875 to 0.1875
- key_weight: bfloat16 [1024, 1024], P('row', 'col'), may hold values from -0.1875 to 0.1875
- value_weight: bfloat16 [1024, 1024], P('row', 'col'), may hold values from -0.1875 to 0.1875
- projection_weight: bfloat16 [2048, 1024], P('col', 'row'), may hold values from -1 to 1
- w_gate: bfloat16 [1024, 3072], P('row', 'col'), may hold values from -0.1875 to 0.1875
- w_up: bfloat16 [1024, 3072], P('row', 'col'), may hold values from -0.1875 to 0.1875
- w_down: bfloat16 [3072, 1024], P('col', 'row'), may hold values from -0.15625 to 0.15625
- attn_gain: float32 [1024], P('row'), may hold values from 0.1 to 1.9
- ffn_gain: float32 [1024], P('row'), may hold values from 0.1 to 1.9
- query_gain: float32 [128], replicated, may hold values from 0.7 to 1.6, as said below
- key_gain: float32 [128], replicated, may hold values from 0.7 to 1.6, as said below
- cotangent: float32 [2048, 1024], P(('dp', 'col'), 'row'), may hold values from -6 to 6
Outputs:
- block_output: float32 [2048, 1024], P(('dp', 'col'), 'row')
- input_grad: float32 [2048, 1024], P(('dp', 'col'), 'row')
- grad_query: float32 [1024, 2048], P('row', 'col')
- grad_key: float32 [1024, 1024], P('row', 'col')
- grad_value: float32 [1024, 1024], P('row', 'col')
- grad_proj: float32 [2048, 1024], P('col', 'row')
- grad_gate: float32 [1024, 3072], P('row', 'col')
- grad_up: float32 [1024, 3072], P('row', 'col')
- grad_down: float32 [3072, 1024], P('col', 'row')
- attn_dgain: float32 [1024], P('row')
- ffn_dgain: float32 [1024], P('row')
- query_dgain: float32 [128], replicated
- key_dgain: float32 [128], replicated
The draws below stay inside these ranges and needn't reach their ends.
Inputs may be any that keep to these rules, and one draw needn't show every extreme that they name: `query_gain`: 128 positive entries. `key_gain`: 128 positive entries.
All inputs are finite; a program needn't handle non-finite values.
Results may differ from the reference program's by a relative error of at most 0.018.
Values may be sent and summed in bfloat16 or wider, within the bound.
No kernel may reach another device: no remote copies, remote signals or barrier semaphores. Data moves between devices by JAX's collectives and lax.ppermute only.
A program may use at most 128 MiB of HBM per device.

```python
import jax
import jax.numpy as jnp
from jax import lax

MODEL_WIDTH = 1024
QUERY_HEADS = 16
KEY_VALUE_HEADS = 8
HEAD_DIMENSION = 128
FF = 3072
SEQUENCE_LENGTH = 256
GROUP_TOK = 1024
TOKENS = 2048
N_DP = 2


def gain_values(key):
    spread = jax.random.normal(key, (HEAD_DIMENSION,), jnp.float32) * 0.15
    return jnp.clip(1.15 + spread, 0.7, 1.6)


def draw_query_gain(key, part):
    return gain_values(jax.random.fold_in(key, 11))


def draw_key_gain(key, part):
    return gain_values(jax.random.fold_in(key, 23))


def shard_levels(key, dims, shards, smallest, top_value):
    level = 1.0
    for axis_at, blocks in shards:
        heights = jax.random.uniform(jax.random.fold_in(jax.random.fold_in(key, 6), axis_at), (blocks,), jnp.float32, smallest / len(shards), top_value / len(shards))
        level = level * jnp.repeat(jnp.exp(heights), dims[axis_at] // blocks).reshape((-1,) + (1,) * (len(dims) - 1 - axis_at))
    return level


def noise(own_key, dims, scale, bound, split=(), kind=jnp.bfloat16):
    level = shard_levels(own_key, dims, split, -0.22, 0.18) if split else 1.0
    array = jax.random.normal(own_key, dims, jnp.float32) * scale * level
    return jnp.minimum(jnp.maximum(array, -bound), bound).astype(kind)


def setup_inputs(seed: int = 0) -> dict:
    splits = jax.random.split(jax.random.key(seed), 14)
    block_input = noise(splits[0], (TOKENS, MODEL_WIDTH), 1.0, 6.0, ((0, 8), (1, 4)))
    query_weight = noise(splits[1], (MODEL_WIDTH, QUERY_HEADS * HEAD_DIMENSION), MODEL_WIDTH ** -0.5, 0.1875, ((0, 4), (1, 4)))
    key_weight = noise(splits[2], (MODEL_WIDTH, KEY_VALUE_HEADS * HEAD_DIMENSION), MODEL_WIDTH ** -0.5, 0.1875, ((0, 4), (1, 4)))
    value_weight = noise(splits[3], (MODEL_WIDTH, KEY_VALUE_HEADS * HEAD_DIMENSION), MODEL_WIDTH ** -0.5, 0.1875, ((0, 4), (1, 4)))
    projection_weight = noise(splits[4], (QUERY_HEADS * HEAD_DIMENSION, MODEL_WIDTH), (QUERY_HEADS * HEAD_DIMENSION // 64) ** -0.5, 1.0, ((0, 4), (1, 4)))
    w_gate = noise(splits[5], (MODEL_WIDTH, FF), MODEL_WIDTH ** -0.5, 0.1875, ((0, 4), (1, 4)))
    w_up = noise(splits[6], (MODEL_WIDTH, FF), MODEL_WIDTH ** -0.5, 0.1875, ((0, 4), (1, 4)))
    w_down = noise(splits[7], (FF, MODEL_WIDTH), (FF // 2) ** -0.5, 0.15625, ((0, 4), (1, 4)))
    attn_gain = jnp.clip(1.0 + 0.18 * jax.random.normal(splits[8], (MODEL_WIDTH,), jnp.float32), 0.1, 1.9)
    ffn_gain = jnp.clip(1.0 + 0.18 * jax.random.normal(splits[9], (MODEL_WIDTH,), jnp.float32), 0.1, 1.9)
    query_gain = draw_query_gain(jax.random.fold_in(splits[13], 71), 0)
    key_gain = draw_key_gain(jax.random.fold_in(splits[13], 71), 0)
    cotangent = noise(splits[12], (TOKENS, MODEL_WIDTH), 1.0, 6.0, ((0, 8), (1, 4)), jnp.float32)
    return {"block_input": block_input, "query_weight": query_weight, "key_weight": key_weight, "value_weight": value_weight, "projection_weight": projection_weight, "w_gate": w_gate, "w_up": w_up, "w_down": w_down, "attn_gain": attn_gain, "ffn_gain": ffn_gain, "query_gain": query_gain, "key_gain": key_gain, "cotangent": cotangent}


epsilon = 1e-06
rope_base = 1000000.0
masked_value = -1e+30

def matrix_product(left, right):
    return jnp.dot(left, right, preferred_element_type=jnp.float32)

def rope_tables(length, head_size):
    places = jnp.arange(length).astype(jnp.float32)
    freqs = rope_base ** (-(jnp.arange(head_size // 2).astype(jnp.float32) * 2.0) / head_size)
    angles = places[:, None] * freqs[None, :]
    angles = jnp.concatenate([angles, angles], 1)
    return (jnp.cos(angles), jnp.sin(angles))

def rotate(values, cos_tab, sin_tab):
    half_dim = values.shape[-1] // 2
    turned = jnp.concatenate([-values[..., half_dim:], values[..., :half_dim]], -1)
    return values * cos_tab + turned * sin_tab

def rotate_back(grads, cos_tab, sin_tab):
    half_dim = grads.shape[-1] // 2
    by_sin = grads * sin_tab
    turned = jnp.concatenate([by_sin[..., half_dim:], -by_sin[..., :half_dim]], -1)
    return grads * cos_tab + turned

def head_norm(values):
    scales = lax.rsqrt(lax.optimization_barrier(jnp.mean(values * values, -1, keepdims=True)) + epsilon)
    return (values * scales, scales)

def head_norm_back(grads, normed, scales, gain):
    reduce_axes = tuple(range(grads.ndim - 1))
    dgain = lax.optimization_barrier(jnp.sum(grads * normed, axis=reduce_axes))
    scaled = grads * gain
    return (scales * (scaled - normed * lax.optimization_barrier(jnp.mean(scaled * normed, -1, keepdims=True))), dgain)

def causal_keep(length):
    row_ids = lax.broadcasted_iota(jnp.int32, (length, length), 0)
    col_ids = lax.broadcasted_iota(jnp.int32, (length, length), 1)
    return row_ids >= col_ids

def masked_scores(query_rot, key_rot):
    factor = query_rot.shape[-1] ** (-0.5)
    scores = jnp.einsum('qgrd,kgd->grqk', query_rot.astype(jnp.float32), key_rot.astype(jnp.float32)) * factor
    return jnp.where(causal_keep(query_rot.shape[0]), scores, masked_value)

def attend(query_rot, key_rot, values):
    scores = masked_scores(query_rot, key_rot)
    row_max = lax.optimization_barrier(jnp.max(scores, -1, keepdims=True))
    exp_scores = jnp.exp(scores - row_max)
    totals = lax.optimization_barrier(jnp.sum(exp_scores, -1, keepdims=True))
    probs_b = (exp_scores / totals).astype(jnp.bfloat16)
    log_sum = row_max + jnp.log(totals)
    outputs = jnp.einsum('grqk,kgd->qgrd', probs_b.astype(jnp.float32), values.astype(jnp.float32))
    return (outputs.astype(jnp.bfloat16), log_sum[..., 0])

def attend_back(query_rot, key_rot, values, outputs, grad_out, log_sum):
    factor = query_rot.shape[-1] ** (-0.5)
    scores = masked_scores(query_rot, key_rot)
    probs = jnp.exp(scores - log_sum[..., None])
    probs_b = probs.astype(jnp.bfloat16)
    grad_f = grad_out.astype(jnp.float32)
    value_rows_gradient = jnp.einsum('grqk,qgrd->kgd', probs_b.astype(jnp.float32), grad_f)
    d_probs = jnp.einsum('qgrd,kgd->grqk', grad_f, values.astype(jnp.float32))
    delta_rows = jnp.transpose(lax.optimization_barrier(jnp.sum(grad_f * outputs.astype(jnp.float32), -1)), (1, 2, 0))
    ds_b = (probs * (d_probs - delta_rows[..., None])).astype(jnp.bfloat16).astype(jnp.float32)
    d_query = jnp.einsum('grqk,kgd->qgrd', ds_b, key_rot.astype(jnp.float32)) * factor
    d_key = jnp.einsum('grqk,qgrd->kgd', ds_b, query_rot.astype(jnp.float32)) * factor
    return (d_query, d_key, value_rows_gradient)

def group_pass(weights, inputs_b, cot):
    query_weight, key_weight, value_weight, projection_weight, w_gate, w_up, w_down, attn_gain, ffn_gain, query_gain, key_gain = weights
    token_rows = inputs_b.shape[0]
    sequence_count = token_rows // SEQUENCE_LENGTH
    query_groups = QUERY_HEADS // KEY_VALUE_HEADS
    cos_tab, sin_tab = rope_tables(SEQUENCE_LENGTH, HEAD_DIMENSION)
    q_cos, q_sin = (cos_tab[:, None, None, :], sin_tab[:, None, None, :])
    k_cos, k_sin = (cos_tab[:, None, :], sin_tab[:, None, :])
    inputs = inputs_b.astype(jnp.float32)
    r_one = lax.rsqrt(lax.optimization_barrier(jnp.mean(inputs * inputs, -1, keepdims=True)) + epsilon)
    n_one = inputs * r_one
    attention_input = (n_one * attn_gain).astype(jnp.bfloat16)
    query_unrotated = matrix_product(attention_input, query_weight).reshape(sequence_count, SEQUENCE_LENGTH, KEY_VALUE_HEADS, query_groups, HEAD_DIMENSION)
    key_unrotated = matrix_product(attention_input, key_weight).reshape(sequence_count, SEQUENCE_LENGTH, KEY_VALUE_HEADS, HEAD_DIMENSION)
    value_input = matrix_product(attention_input, value_weight).astype(jnp.bfloat16).reshape(sequence_count, SEQUENCE_LENGTH, KEY_VALUE_HEADS, HEAD_DIMENSION)
    q_norm, q_scale = head_norm(query_unrotated)
    k_norm, k_scale = head_norm(key_unrotated)
    q_rot = rotate(q_norm * query_gain, q_cos, q_sin).astype(jnp.bfloat16)
    k_rot = rotate(k_norm * key_gain, k_cos, k_sin).astype(jnp.bfloat16)
    attn_out, log_sum = lax.map(lambda triple: attend(triple[0], triple[1], triple[2]), (q_rot, k_rot, value_input))
    o_flat = attn_out.reshape(token_rows, QUERY_HEADS * HEAD_DIMENSION)
    hidden_one = inputs + matrix_product(o_flat, projection_weight)
    r_two = lax.rsqrt(lax.optimization_barrier(jnp.mean(hidden_one * hidden_one, -1, keepdims=True)) + epsilon)
    n_two = hidden_one * r_two
    b_in = (n_two * ffn_gain).astype(jnp.bfloat16)
    gate_val = matrix_product(b_in, w_gate)
    up_val = matrix_product(b_in, w_up)
    sigmoid_gate = jax.nn.sigmoid(gate_val)
    act_val = gate_val * sigmoid_gate
    m_in = (act_val * up_val).astype(jnp.bfloat16)
    block_out = hidden_one + matrix_product(m_in, w_down)
    dy_b = cot.astype(jnp.bfloat16)
    g_down = matrix_product(m_in.T, dy_b)
    d_act = matrix_product(dy_b, w_down.T)
    d_gate = (d_act * up_val * sigmoid_gate * (1.0 + gate_val * (1.0 - sigmoid_gate))).astype(jnp.bfloat16)
    d_up = (d_act * act_val).astype(jnp.bfloat16)
    g_gate = matrix_product(b_in.T, d_gate)
    g_up = matrix_product(b_in.T, d_up)
    d_bin = matrix_product(d_gate, w_gate.T) + matrix_product(d_up, w_up.T)
    ffn_part = lax.optimization_barrier(jnp.sum(d_bin * n_two, 0))
    s_two = d_bin * ffn_gain
    d_hidden = cot + r_two * (s_two - n_two * lax.optimization_barrier(jnp.mean(s_two * n_two, -1, keepdims=True)))
    hidden_block_gradient = d_hidden.astype(jnp.bfloat16)
    g_proj = matrix_product(o_flat.T, hidden_block_gradient)
    output_gradient = matrix_product(hidden_block_gradient, projection_weight.T).astype(jnp.bfloat16).reshape(sequence_count, SEQUENCE_LENGTH, KEY_VALUE_HEADS, query_groups, HEAD_DIMENSION)
    d_qrot, d_krot, value_rows_gradient = lax.map(lambda items: attend_back(items[0], items[1], items[2], items[3], items[4], items[5]), (q_rot, k_rot, value_input, attn_out, output_gradient, log_sum))
    d_qn, qg_part = head_norm_back(rotate_back(d_qrot, q_cos, q_sin), q_norm, q_scale, query_gain)
    normed_key_gradient, kg_part = head_norm_back(rotate_back(d_krot, k_cos, k_sin), k_norm, k_scale, key_gain)
    d_q = d_qn.reshape(token_rows, QUERY_HEADS * HEAD_DIMENSION).astype(jnp.bfloat16)
    key_gradient = normed_key_gradient.reshape(token_rows, KEY_VALUE_HEADS * HEAD_DIMENSION).astype(jnp.bfloat16)
    value_gradient = value_rows_gradient.reshape(token_rows, KEY_VALUE_HEADS * HEAD_DIMENSION).astype(jnp.bfloat16)
    g_query = matrix_product(attention_input.T, d_q)
    g_key = matrix_product(attention_input.T, key_gradient)
    g_value = matrix_product(attention_input.T, value_gradient)
    d_ain = matrix_product(d_q, query_weight.T) + matrix_product(key_gradient, key_weight.T) + matrix_product(value_gradient, value_weight.T)
    attn_part = lax.optimization_barrier(jnp.sum(d_ain * n_one, 0))
    s_one = d_ain * attn_gain
    in_grad = d_hidden + r_one * (s_one - n_one * lax.optimization_barrier(jnp.mean(s_one * n_one, -1, keepdims=True)))
    grads = (g_query, g_key, g_value, g_proj, g_gate, g_up, g_down, attn_part, ffn_part, qg_part, kg_part)
    return (block_out, in_grad, grads)

def reference(block_input, query_weight, key_weight, value_weight, projection_weight, w_gate, w_up, w_down, attn_gain, ffn_gain, query_gain, key_gain, cotangent):
    weights = (query_weight, key_weight, value_weight, projection_weight, w_gate, w_up, w_down, attn_gain, ffn_gain, query_gain, key_gain)
    in_groups = block_input.reshape(N_DP, GROUP_TOK, MODEL_WIDTH)
    cot_groups = cotangent.reshape(N_DP, GROUP_TOK, MODEL_WIDTH)
    start = tuple((jnp.zeros(item.shape, jnp.float32) for item in weights))

    def advance(carry, pair):
        block_out, in_grad, grads = group_pass(weights, pair[0], pair[1])
        return (tuple((left + right for left, right in zip(carry, grads))), (block_out, in_grad))
    totals, stacked = lax.scan(advance, start, (in_groups, cot_groups))
    block_output = stacked[0].reshape(TOKENS, MODEL_WIDTH)
    input_grad = stacked[1].reshape(TOKENS, MODEL_WIDTH)
    return (block_output, input_grad, totals[0], totals[1], totals[2], totals[3], totals[4], totals[5], totals[6], totals[7], totals[8], totals[9], totals[10])
```

```python
import functools

import jax
import jax.numpy as jnp
import numpy as np
from jax import lax
from jax.experimental import pallas as pl
from jax.experimental.pallas import tpu as pltpu
from jax.sharding import PartitionSpec as P

MODEL_WIDTH = 1024
HEAD_DIMENSION = 128
SEQUENCE_LENGTH = 256
GROUPS = 2

epsilon = 1e-06
rope_base = 1000000.0
masked_value = -1e30

F32 = jnp.float32
BF16 = jnp.bfloat16
BLK = 256
ROWS = 4
SWAP = (0, 2, 1, 3)


def rope_tables():
    places = np.arange(SEQUENCE_LENGTH, dtype=np.float32)
    half = HEAD_DIMENSION // 2
    freqs = np.float32(rope_base) ** (
        -(np.arange(half, dtype=np.float32) * np.float32(2.0)) / np.float32(HEAD_DIMENSION)
    )
    angles = places[:, None] * freqs[None, :].astype(np.float32)
    cos, sin = np.cos(angles), np.sin(angles)
    return (
        np.concatenate([cos, cos], 1).astype(np.float32),
        np.concatenate([-sin, sin], 1).astype(np.float32),
    )


def dot(left, right):
    return jnp.dot(left, right, preferred_element_type=F32)


def dot_nt(left, right):
    return lax.dot_general(left, right, (((1,), (1,)), ((), ())), preferred_element_type=F32)


def dot_tn(left, right):
    return lax.dot_general(left, right, (((0,), (0,)), ((), ())), preferred_element_type=F32)


def call(body, outs, args, scratch=(), flops=0, smem=None):
    vm = pl.BlockSpec(memory_space=pltpu.VMEM)
    in_specs = [vm] * len(args)
    if smem is not None:
        in_specs = [pl.BlockSpec(memory_space=pltpu.SMEM)] + in_specs
        args = (smem,) + tuple(args)
    moved = sum(int(np.prod(a.shape)) * a.dtype.itemsize for a in list(args) + list(outs))
    return pl.pallas_call(
        body,
        out_shape=[jax.ShapeDtypeStruct(o.shape, o.dtype) for o in outs],
        in_specs=in_specs,
        out_specs=[vm] * len(outs),
        scratch_shapes=list(scratch),
        compiler_params=pltpu.CompilerParams(vmem_limit_bytes=40 << 20),
        cost_estimate=pl.CostEstimate(flops=flops, bytes_accessed=moved, transcendentals=0),
    )(*args)


def sds(shape, dtype):
    return jax.ShapeDtypeStruct(shape, dtype)


def split3(values):
    high = values.astype(BF16).astype(F32)
    rest = values - high
    mid = rest.astype(BF16).astype(F32)
    return high, mid, rest - mid


def pack_qkv(wq, wk, wv, ga, gf, out):
    nq, nk = wq.shape[1], wk.shape[1]
    out[0:BLK, 0:nq] = wq[...]
    out[0:BLK, nq : nq + nk] = wk[...]
    out[0:BLK, nq + nk :] = wv[...]
    rows = split3(ga[...]) + split3(gf[...])
    ids = lax.broadcasted_iota(jnp.int32, (16, BLK), 0)
    extra = jnp.zeros((16, BLK), F32)
    for n, row in enumerate(rows):
        extra = jnp.where(ids == n, jnp.broadcast_to(row, (16, BLK)), extra)
    out[BLK : BLK + 16, :] = jnp.zeros((16, out.shape[1]), BF16)
    out[BLK : BLK + 16, 0:BLK] = extra.astype(BF16)


def pack_ffn(wg, wu, wd, out):
    nf = wg.shape[1]
    out[:, 0:nf] = wg[...]
    out[:, nf : 2 * nf] = wu[...]
    for i in range(nf // BLK):
        out[:, 2 * nf + i * BLK : 2 * nf + (i + 1) * BLK] = wd[i * BLK : (i + 1) * BLK, :]


def rope(values, cos, sin):
    return values * cos + pltpu.roll(values, HEAD_DIMENSION // 2, 1) * sin


def rope_back(values, cos, sin):
    return values * cos + pltpu.roll(values * sin, HEAD_DIMENSION // 2, 1)


def head(ref, n):
    return ref[:, n * HEAD_DIMENSION : (n + 1) * HEAD_DIMENSION]


def attn_forward(
    ids, x0, x1, x2, x3, q0, q1, q2, q3, cos_r, sin_r, qg_r, kg_r,
    x_out, a_out, gains, o_out, qn_out, kn_out, sc_out, qr_out, kr_out, v_out, pr_out, qkv,
):
    s1 = ids[2]
    qs = (q0, q1, q2, q3)
    for k, ref in enumerate((x0, x1, x2, x3)):
        x_out[s1 ^ SWAP[k]] = ref[...]
    total = jnp.zeros((BLK, 1), F32)
    for p in range(ROWS):
        x = x_out[p].astype(F32)
        total = total + jnp.sum(x * x, -1, keepdims=True)
        extra = qs[p][BLK : BLK + 16, 0:BLK].astype(F32)
        gains[p : p + 1, :] = extra[0:1] + extra[1:2] + extra[2:3]
        gains[ROWS + p : ROWS + p + 1, :] = extra[3:4] + extra[4:5] + extra[5:6]
    r_one = lax.rsqrt(total / MODEL_WIDTH + epsilon)
    for p in range(ROWS):
        a_out[p] = ((x_out[p].astype(F32) * r_one) * gains[p : p + 1, :]).astype(BF16)
    for p in range(ROWS):
        part = dot(a_out[p], qs[p][0:BLK, :])
        if p == 0:
            qkv[...] = part
        else:
            qkv[...] += part
    cos, sin = cos_r[...], sin_r[...]
    nkv = kn_out.shape[1] // HEAD_DIMENSION
    nq = qn_out.shape[1] // HEAD_DIMENSION
    lanes = lax.broadcasted_iota(jnp.int32, (BLK, HEAD_DIMENSION), 1)
    packed = jnp.zeros((BLK, HEAD_DIMENSION), F32)
    for n in range(nq + nkv):
        raw = head(qkv, n)
        scale = lax.rsqrt(jnp.mean(raw * raw, -1, keepdims=True) + epsilon)
        packed = jnp.where(lanes == n, scale, packed)
        normed = raw * scale
        cols = slice(n * HEAD_DIMENSION, (n + 1) * HEAD_DIMENSION)
        if n < nq:
            qn_out[:, cols] = normed
            qr_out[:, cols] = rope(normed * qg_r[...], cos, sin).astype(BF16)
        else:
            cols = slice((n - nq) * HEAD_DIMENSION, (n - nq + 1) * HEAD_DIMENSION)
            kn_out[:, cols] = normed
            kr_out[:, cols] = rope(normed * kg_r[...], cos, sin).astype(BF16)
    sc_out[...] = packed
    for n in range(nkv):
        v_out[:, n * HEAD_DIMENSION : (n + 1) * HEAD_DIMENSION] = head(qkv, nq + nkv + n).astype(BF16)
    keep = lax.broadcasted_iota(jnp.int32, (BLK, BLK), 0) >= lax.broadcasted_iota(
        jnp.int32, (BLK, BLK), 1
    )
    factor = HEAD_DIMENSION ** (-0.5)
    for n in range(nq):
        g = n // GROUPS
        scores = jnp.where(keep, dot_nt(head(qr_out, n), head(kr_out, g)) * factor, masked_value)
        top = jnp.max(scores, -1, keepdims=True)
        weights = jnp.exp(scores - top)
        probs = weights / jnp.sum(weights, -1, keepdims=True)
        pr_out[n] = probs
        o_out[:, n * HEAD_DIMENSION : (n + 1) * HEAD_DIMENSION] = dot(
            probs.astype(BF16), head(v_out, g)
        ).astype(BF16)


def project(ids, o, w0, w1, w2, w3, s0, s1, s2, s3, place):
    for p, w in enumerate((w0, w1, w2, w3)):
        place[p] = dot(o[...], w[...]).astype(BF16)
    for k, slot in enumerate((s0, s1, s2, s3)):
        slot[...] = place[ids[1] ^ k]


def ffn(
    ids, t0, t1, t2, t3, x, y0, y1, y2, y3, f0, f1, f2, f3, gains,
    s0, s1, s2, s3, b_out, dy_out, m_out, d_out, h_out, gu, da, place,
):
    c, swapped = ids[1], ids[2]
    fs = (f0, f1, f2, f3)
    nf = m_out.shape[1]
    for k, ref in enumerate((t0, t1, t2, t3)):
        h_out[c ^ k] = ref[...].astype(F32)
    for k, ref in enumerate((y0, y1, y2, y3)):
        dy_out[swapped ^ SWAP[k]] = ref[...]
    total = jnp.zeros((BLK, 1), F32)
    for p in range(ROWS):
        h = h_out[p] + x[p].astype(F32)
        h_out[p] = h
        total = total + jnp.sum(h * h, -1, keepdims=True)
    r_two = lax.rsqrt(total / MODEL_WIDTH + epsilon)
    for p in range(ROWS):
        b_out[p] = ((h_out[p] * r_two) * gains[ROWS + p : ROWS + p + 1, :]).astype(BF16)
    for p in range(ROWS):
        part = dot(b_out[p], fs[p][:, 0 : 2 * nf])
        if p == 0:
            gu[...] = part
        else:
            gu[...] += part
    for i in range(nf // BLK):
        at = slice(2 * nf + i * BLK, 2 * nf + (i + 1) * BLK)
        cols = slice(i * BLK, (i + 1) * BLK)
        acc = dot_nt(dy_out[0], fs[0][:, at])
        for p in range(1, ROWS):
            acc = acc + dot_nt(dy_out[p], fs[p][:, at])
        da[:, cols] = acc
    for i in range(nf // BLK):
        cols = slice(i * BLK, (i + 1) * BLK)
        ups = slice(nf + i * BLK, nf + (i + 1) * BLK)
        gate, up, d_act = gu[:, cols], gu[:, ups], da[:, cols]
        sig = 1.0 / (1.0 + jnp.exp(-gate))
        act = gate * sig
        m_out[:, cols] = (act * up).astype(BF16)
        d_out[:, cols] = (d_act * up * sig * (1.0 + gate * (1.0 - sig))).astype(BF16)
        d_out[:, ups] = (d_act * act).astype(BF16)
    for p in range(ROWS):
        place[p] = dot_nt(d_out[...], fs[p][:, 0 : 2 * nf]).astype(BF16)
    for k, slot in enumerate((s0, s1, s2, s3)):
        slot[...] = place[c ^ k]


def down(ids, m, f0, f1, f2, f3, h, s0, s1, s2, s3, h_own, place):
    nf = m.shape[1]
    for p, f in enumerate((f0, f1, f2, f3)):
        acc = jnp.zeros((BLK, BLK), F32)
        for i in range(nf // BLK):
            at = slice(2 * nf + i * BLK, 2 * nf + (i + 1) * BLK)
            acc = acc + dot(m[:, i * BLK : (i + 1) * BLK], f[:, at])
        place[p] = acc.astype(BF16)
    for k, slot in enumerate((s0, s1, s2, s3)):
        slot[...] = place[ids[1] ^ k]
    h_own[...] = h[ids[1]]


def ffn_grads(b, d, m, dy, send, keep):
    nf = m.shape[1]
    for p in range(ROWS):
        out = keep if p < 2 else send
        rows = slice((p % 2) * BLK, (p % 2 + 1) * BLK)
        out[rows, 0 : 2 * nf] = dot_tn(b[p], d[...]).astype(BF16)
        for i in range(nf // BLK):
            at = slice(2 * nf + i * BLK, 2 * nf + (i + 1) * BLK)
            out[rows, at] = dot_tn(m[:, i * BLK : (i + 1) * BLK], dy[p]).astype(BF16)


def attn_grads(a, d, o, dh, send, keep):
    nd = d.shape[1]
    for p in range(ROWS):
        out = keep if p < 2 else send
        rows = slice((p % 2) * BLK, (p % 2 + 1) * BLK)
        out[rows, 0:nd] = dot_tn(a[p], d[...]).astype(BF16)
        for i in range(o.shape[1] // BLK):
            at = slice(nd + i * BLK, nd + (i + 1) * BLK)
            out[rows, at] = dot_tn(o[:, i * BLK : (i + 1) * BLK], dh[p]).astype(BF16)


def attn_backward(
    ids, t0, t1, t2, t3, h, dy, gains, w0, w1, w2, w3, x, q0, q1, q2, q3,
    o, qn, kn, sc, qr, kr, v, pr, cos_r, sin_r, qg_r, kg_r,
    s0, s1, s2, s3, dhb, d_qkv, dh_own, sums, dh, part,
):
    r, c = ids[0], ids[1]
    for k, ref in enumerate((t0, t1, t2, t3)):
        dh[c ^ k] = ref[...].astype(F32)
    total = jnp.zeros((BLK, 1), F32)
    for p in range(ROWS):
        total = total + jnp.sum(h[p] * h[p], -1, keepdims=True)
    r_two = lax.rsqrt(total / MODEL_WIDTH + epsilon)
    sums[...] = jnp.zeros(sums.shape, F32)
    first = (c == 0).astype(F32)
    inner = jnp.zeros((BLK, 1), F32)
    for p in range(ROWS):
        n_two = h[p] * r_two
        term = dh[p] * n_two
        sums[pl.ds(ROWS + (r ^ SWAP[p]), 1), :] = jnp.sum(term, 0, keepdims=True) * first
        inner = inner + jnp.sum(term * gains[ROWS + p : ROWS + p + 1, :], -1, keepdims=True)
    inner = inner / MODEL_WIDTH
    for p in range(ROWS):
        n_two = h[p] * r_two
        s_two = dh[p] * gains[ROWS + p : ROWS + p + 1, :]
        out = dy[p].astype(F32) + r_two * (s_two - n_two * inner)
        dh[p] = out
        dhb[p] = out.astype(BF16)
    dh_own[...] = dh[c]
    nq, nkv = qn.shape[1] // HEAD_DIMENSION, kn.shape[1] // HEAD_DIMENSION
    d_o = dot_nt(dhb[0], w0[...])
    for p, w in ((1, w1), (2, w2), (3, w3)):
        d_o = d_o + dot_nt(dhb[p], w[...])
    d_o = d_o.astype(BF16)
    cos, sin = cos_r[...], sin_r[...]
    factor = HEAD_DIMENSION ** (-0.5)
    q_sum = jnp.zeros((1, HEAD_DIMENSION), F32)
    k_sum = jnp.zeros((1, HEAD_DIMENSION), F32)

    def norm_back(grad, normed, scale, gain):
        gained = grad * gain
        return scale * (gained - normed * jnp.mean(gained * normed, -1, keepdims=True))

    for g in range(nkv):
        d_k = jnp.zeros((BLK, HEAD_DIMENSION), F32)
        d_v = jnp.zeros((BLK, HEAD_DIMENSION), F32)
        for n in range(g * GROUPS, (g + 1) * GROUPS):
            grad = d_o[:, n * HEAD_DIMENSION : (n + 1) * HEAD_DIMENSION]
            delta = jnp.sum(grad.astype(F32) * head(o, n).astype(F32), -1, keepdims=True)
            probs = pr[n]
            d_v = d_v + dot_tn(probs.astype(BF16), grad)
            d_s = (probs * (dot_nt(grad, head(v, g)) - delta)).astype(BF16)
            d_q = dot(d_s, head(kr, g)) * factor
            d_k = d_k + dot_tn(d_s, head(qr, n))
            e_q = rope_back(d_q, cos, sin)
            normed = head(qn, n)
            q_sum = q_sum + jnp.sum(e_q * normed, 0, keepdims=True)
            d_qkv[:, n * HEAD_DIMENSION : (n + 1) * HEAD_DIMENSION] = norm_back(
                e_q, normed, sc[:, n : n + 1], qg_r[...]
            ).astype(BF16)
        e_k = rope_back(d_k * factor, cos, sin)
        normed = head(kn, g)
        k_sum = k_sum + jnp.sum(e_k * normed, 0, keepdims=True)
        at = (nq + g) * HEAD_DIMENSION
        d_qkv[:, at : at + HEAD_DIMENSION] = norm_back(
            e_k, normed, sc[:, nq + g : nq + g + 1], kg_r[...]
        ).astype(BF16)
        at = (nq + nkv + g) * HEAD_DIMENSION
        d_qkv[:, at : at + HEAD_DIMENSION] = d_v.astype(BF16)
    sums[8:9, 0:HEAD_DIMENSION] = q_sum
    sums[8:9, HEAD_DIMENSION : 2 * HEAD_DIMENSION] = k_sum
    total = jnp.zeros((BLK, 1), F32)
    for p in range(ROWS):
        xf = x[p].astype(F32)
        total = total + jnp.sum(xf * xf, -1, keepdims=True)
    r_one = lax.rsqrt(total / MODEL_WIDTH + epsilon)
    inner = jnp.zeros((BLK, 1), F32)
    for p, q in enumerate((q0, q1, q2, q3)):
        d_a = dot_nt(d_qkv[...], q[0:BLK, :])
        term = d_a * (x[p].astype(F32) * r_one)
        sums[pl.ds(r ^ SWAP[p], 1), :] = jnp.sum(term, 0, keepdims=True)
        inner = inner + jnp.sum(term * gains[p : p + 1, :], -1, keepdims=True)
        part[p] = d_a.astype(BF16)
    row = jnp.transpose(jnp.broadcast_to(inner, (BLK, 128)))[0:16, :]
    high = row.astype(BF16).astype(F32)
    ids16 = lax.broadcasted_iota(jnp.int32, (16, BLK), 0)
    tail = jnp.where(ids16 == 0, high, jnp.where(ids16 == 1, row - high, 0.0)).astype(BF16)
    for k, slot in enumerate((s0, s1, s2, s3)):
        slot[0:BLK, :] = part[c ^ k]
        slot[BLK : BLK + 16, :] = tail


def finish(ids, t0, t1, t2, t3, dh_own, x, gains, out):
    c = ids[1]
    refs = (t0, t1, t2, t3)
    d_a = refs[0][0:BLK, :].astype(F32)
    tail = refs[0][BLK : BLK + 16, :].astype(F32)
    for ref in refs[1:]:
        d_a = d_a + ref[0:BLK, :].astype(F32)
        tail = tail + ref[BLK : BLK + 16, :].astype(F32)
    row = jnp.broadcast_to(tail[0:1] + tail[1:2], (128, BLK))
    inner = jnp.transpose(row)[:, 0:1] / MODEL_WIDTH
    total = jnp.zeros((BLK, 1), F32)
    for p in range(ROWS):
        xf = x[p].astype(F32)
        total = total + jnp.sum(xf * xf, -1, keepdims=True)
    r_one = lax.rsqrt(total / MODEL_WIDTH + epsilon)
    gain = gains[pl.ds(c, 1), :]
    n_one = x[c].astype(F32) * r_one
    out[...] = (dh_own[...] + r_one * (d_a * gain - n_one * inner)).astype(BF16)


def row_swap(values, bit):
    return lax.ppermute(values, "row", [(i, i ^ bit) for i in range(ROWS)])


def col_swap(values, bit):
    return lax.ppermute(values, "col", [(i, i ^ bit) for i in range(ROWS)])


def all_of_row(shard):
    other = row_swap(shard, 2)
    return (shard, other, row_swap(shard, 1), row_swap(other, 1))


def to_sequence(block):
    return [
        lax.ppermute(
            block, ("row", "col"),
            [(r * ROWS + c, c * ROWS + (r ^ k)) for r in range(ROWS) for c in range(ROWS)],
        )
        for k in range(ROWS)
    ]


def to_owner(block):
    return lax.ppermute(
        block, ("row", "col"),
        [(r * ROWS + c, (r ^ SWAP[c]) * ROWS + r) for r in range(ROWS) for c in range(ROWS)],
    )


def scatter_col(slots):
    return [slots[0]] + [col_swap(slots[k], k) for k in range(1, ROWS)]


def gather_col(block):
    return [block] + [col_swap(block, k) for k in range(1, ROWS)]


def add_all(parts):
    total = parts[0].astype(F32)
    for item in parts[1:]:
        total = total + item.astype(F32)
    return total


def per_device(
    n_dp, block_input, query_weight, key_weight, value_weight, projection_weight,
    w_gate, w_up, w_down, attn_gain, ffn_gain, query_gain, key_gain, cotangent,
):
    width_q, width_kv, width_ff = query_weight.shape[1], key_weight.shape[1], w_gate.shape[1]
    width_qkv = width_q + 2 * width_kv
    nq = width_q // HEAD_DIMENSION
    r, c = lax.axis_index("row"), lax.axis_index("col")
    rc = r ^ c
    ids = jnp.stack([r, c, ((rc & 1) << 1) | (rc >> 1)]).astype(jnp.int32)
    cos_np, sin_np = rope_tables()
    cos, sin = jnp.asarray(cos_np), jnp.asarray(sin_np)
    qg, kg = query_gain.reshape(1, -1), key_gain.reshape(1, -1)
    blocks = (ROWS, BLK, BLK)
    slot = sds((BLK, BLK), BF16)

    xs = to_sequence(block_input)
    (msg_q,) = call(
        pack_qkv, [sds((BLK + 16, width_qkv), BF16)],
        (query_weight, key_weight, value_weight, attn_gain.reshape(1, -1), ffn_gain.reshape(1, -1)),
    )
    q_all = all_of_row(msg_q)
    p_all = all_of_row(projection_weight)
    (msg_f,) = call(pack_ffn, [sds((BLK, 3 * width_ff), BF16)], (w_gate, w_up, w_down))
    f_all = all_of_row(msg_f)
    ys = to_sequence(cotangent.astype(BF16))

    x_full, a_full, gains, o, qn, kn, sc, qr, kr, v, pr = call(
        attn_forward,
        [
            sds(blocks, BF16), sds(blocks, BF16), sds((8, BLK), F32), sds((BLK, width_q), BF16),
            sds((BLK, width_q), F32), sds((BLK, width_kv), F32), sds((BLK, HEAD_DIMENSION), F32),
            sds((BLK, width_q), BF16), sds((BLK, width_kv), BF16), sds((BLK, width_kv), BF16),
            sds((nq, BLK, BLK), F32),
        ],
        (*xs, *q_all, cos, sin, qg, kg), [pltpu.VMEM((BLK, width_qkv), F32)],
        2 * BLK * MODEL_WIDTH * width_qkv, ids,
    )
    slots = call(
        project, [slot] * ROWS, (o, *p_all), [pltpu.VMEM(blocks, BF16)],
        2 * BLK * MODEL_WIDTH * width_q, ids,
    )
    h_sum = add_all(scatter_col(slots)).astype(BF16)
    h_parts = gather_col(h_sum)
    *slots, b_full, dy_full, m, d_gu, h_full = call(
        ffn,
        [slot] * ROWS
        + [
            sds(blocks, BF16), sds(blocks, BF16), sds((BLK, width_ff), BF16),
            sds((BLK, 2 * width_ff), BF16), sds(blocks, F32),
        ],
        (*h_parts, x_full, *ys, *f_all, gains),
        [
            pltpu.VMEM((BLK, 2 * width_ff), F32), pltpu.VMEM((BLK, width_ff), F32),
            pltpu.VMEM(blocks, BF16),
        ],
        10 * BLK * MODEL_WIDTH * width_ff, ids,
    )
    b_sum = add_all(scatter_col(slots)).astype(BF16)
    b_parts = gather_col(b_sum)

    f_send, f_keep = call(
        ffn_grads, [sds((2 * BLK, 3 * width_ff), BF16)] * 2, (b_full, d_gu, m, dy_full),
        (), 6 * BLK * MODEL_WIDTH * width_ff,
    )
    *slots, h_own = call(
        down, [slot] * ROWS + [sds((BLK, BLK), F32)], (m, *f_all, h_full),
        [pltpu.VMEM(blocks, BF16)], 2 * BLK * MODEL_WIDTH * width_ff, ids,
    )
    y_own = (h_own + add_all(scatter_col(slots))).astype(BF16)
    block_output = to_owner(y_own).astype(F32)

    *slots, dh_full, d_qkv, dh_own, sums = call(
        attn_backward,
        [sds((BLK + 16, BLK), BF16)] * ROWS
        + [
            sds(blocks, BF16), sds((BLK, width_qkv), BF16), sds((BLK, BLK), F32),
            sds((16, BLK), F32),
        ],
        (*b_parts, h_full, dy_full, gains, *p_all, x_full, *q_all,
         o, qn, kn, sc, qr, kr, v, pr, cos, sin, qg, kg),
        [pltpu.VMEM(blocks, F32), pltpu.VMEM(blocks, BF16)],
        2 * BLK * MODEL_WIDTH * (width_qkv + width_q) + 10 * BLK * BLK * width_q, ids,
    )
    a_parts = scatter_col(slots)
    a_send, a_keep = call(
        attn_grads, [sds((2 * BLK, width_qkv + width_q), BF16)] * 2, (a_full, d_qkv, o, dh_full),
        (), 2 * BLK * MODEL_WIDTH * (width_qkv + width_q),
    )
    (in_own,) = call(finish, [slot], (*a_parts, dh_own, x_full, gains), (), 0, ids)
    input_grad = to_owner(in_own).astype(F32)

    def reduce_grad(send, keep):
        got = row_swap(send, 1)
        mine = keep[0:BLK].astype(F32) + got[0:BLK].astype(F32)
        theirs = (keep[BLK:].astype(F32) + got[BLK:].astype(F32)).astype(BF16)
        total = (mine + row_swap(theirs, 2).astype(F32)).astype(BF16)
        if n_dp == 2:
            return total.astype(F32) + lax.ppermute(total, "dp", [(0, 1), (1, 0)]).astype(F32)
        return lax.psum(total, "dp").astype(F32)

    g_f = reduce_grad(f_send, f_keep)
    g_a = reduce_grad(a_send, a_keep)

    for bit in (1, 2):
        sums = sums + col_swap(sums, bit)
    for bit in (1, 2):
        sums = sums + row_swap(sums, bit)
    if n_dp == 2:
        sums = sums + lax.ppermute(sums, "dp", [(0, 1), (1, 0)])
    else:
        sums = lax.psum(sums, "dp")
    attn_dgain = lax.dynamic_slice_in_dim(sums, r, 1, 0)[0]
    ffn_dgain = lax.dynamic_slice_in_dim(sums, ROWS + r, 1, 0)[0]
    slabs = lambda values: jnp.concatenate(
        [values[:, i * BLK : (i + 1) * BLK] for i in range(values.shape[1] // BLK)], 0
    )
    return (
        block_output,
        input_grad,
        g_a[:, :width_q],
        g_a[:, width_q : width_q + width_kv],
        g_a[:, width_q + width_kv : width_qkv],
        slabs(g_a[:, width_qkv:]),
        g_f[:, :width_ff],
        g_f[:, width_ff : 2 * width_ff],
        slabs(g_f[:, 2 * width_ff :]),
        attn_dgain,
        ffn_dgain,
        sums[8, :HEAD_DIMENSION],
        sums[8, HEAD_DIMENSION:],
    )


def solution(mesh):
    tokens = P(("dp", "col"), "row")
    return jax.shard_map(
        functools.partial(per_device, mesh.shape["dp"]),
        mesh=mesh,
        in_specs=(
            tokens, P("row", "col"), P("row", "col"), P("row", "col"), P("col", "row"),
            P("row", "col"), P("row", "col"), P("col", "row"), P("row"), P("row"), P(), P(), tokens,
        ),
        out_specs=(
            tokens, tokens, P("row", "col"), P("row", "col"), P("row", "col"), P("col", "row"),
            P("row", "col"), P("row", "col"), P("col", "row"), P("row"), P("row"), P(), P(),
        ),
        check_vma=False,
    )
```

```python
import functools

import jax
import jax.numpy as jnp
import numpy as np
from jax import lax
from jax.experimental import pallas as pl
from jax.experimental.pallas import tpu as pltpu
from jax.sharding import PartitionSpec as P

MODEL_WIDTH = 1024
HEAD_DIMENSION = 128
SEQUENCE_LENGTH = 256
GROUPS = 2

epsilon = 1e-06
rope_base = 1000000.0
masked_value = -1e30

F32 = jnp.float32
BF16 = jnp.bfloat16
BLK = 256
ROWS = 4
SWAP = (0, 2, 1, 3)


def rope_tables():
    places = np.arange(SEQUENCE_LENGTH, dtype=np.float32)
    half = HEAD_DIMENSION // 2
    freqs = np.float32(rope_base) ** (
        -(np.arange(half, dtype=np.float32) * np.float32(2.0)) / np.float32(HEAD_DIMENSION)
    )
    angles = places[:, None] * freqs[None, :].astype(np.float32)
    cos, sin = np.cos(angles), np.sin(angles)
    return (
        np.concatenate([cos, cos], 1).astype(np.float32),
        np.concatenate([-sin, sin], 1).astype(np.float32),
    )


def dot(left, right):
    return jnp.dot(left, right, preferred_element_type=F32)


def dot_nt(left, right):
    return lax.dot_general(left, right, (((1,), (1,)), ((), ())), preferred_element_type=F32)


def dot_tn(left, right):
    return lax.dot_general(left, right, (((0,), (0,)), ((), ())), preferred_element_type=F32)


def call(body, outs, args, scratch=(), flops=0, smem=None, anywhere=()):
    vm = pl.BlockSpec(memory_space=pltpu.VMEM)
    in_specs = [
        pl.BlockSpec(memory_space=pltpu.HBM) if n in anywhere else vm for n in range(len(args))
    ]
    if smem is not None:
        in_specs = [pl.BlockSpec(memory_space=pltpu.SMEM)] + in_specs
        args = (smem,) + tuple(args)
    moved = sum(int(np.prod(a.shape)) * a.dtype.itemsize for a in list(args) + list(outs))
    return pl.pallas_call(
        body,
        out_shape=[jax.ShapeDtypeStruct(o.shape, o.dtype) for o in outs],
        in_specs=in_specs,
        out_specs=[vm] * len(outs),
        scratch_shapes=list(scratch),
        compiler_params=pltpu.CompilerParams(vmem_limit_bytes=16 << 20),
        cost_estimate=pl.CostEstimate(flops=flops, bytes_accessed=moved, transcendentals=0),
    )(*args)


def sds(shape, dtype):
    return jax.ShapeDtypeStruct(shape, dtype)


def split3(values):
    high = values.astype(BF16).astype(F32)
    rest = values - high
    mid = rest.astype(BF16).astype(F32)
    return high, mid, rest - mid


def copy_all(pairs, sems):
    copies = [pltpu.make_async_copy(src, dst, sems.at[n]) for n, (src, dst) in enumerate(pairs)]
    for item in copies:
        item.start()
    return copies


def pack_attn(wq, wk, wv, wp, x, dy, ga, gf, out, both, wide, sems):
    nq, nk = wq.shape[1], wk.shape[1]
    pairs = [
        (wq, out.at[0:BLK, 0:nq]),
        (wk, out.at[0:BLK, nq : nq + nk]),
        (wv, out.at[0:BLK, nq + nk : nq + 2 * nk]),
        (x, both.at[0:BLK, :]),
        (dy, wide),
    ]
    for i in range(nq // BLK):
        at = nq + 2 * nk + i * BLK
        pairs.append((wp.at[i * BLK : (i + 1) * BLK, :], out.at[0:BLK, at : at + BLK]))
    copies = copy_all(pairs, sems)
    rows = split3(ga[...]) + split3(gf[...])
    ids = lax.broadcasted_iota(jnp.int32, (16, BLK), 0)
    extra = jnp.zeros((16, BLK), F32)
    for n, row in enumerate(rows):
        extra = jnp.where(ids == n, jnp.broadcast_to(row, (16, BLK)), extra)
    out[BLK : BLK + 16, :] = jnp.zeros((16, out.shape[1]), BF16)
    out[BLK : BLK + 16, 0:BLK] = extra.astype(BF16)
    for item in copies:
        item.wait()
    both[BLK:, :] = wide[...].astype(BF16)


def pack_ffn(wg, wu, wd, out, sems):
    nf = wg.shape[1]
    pairs = [(wg, out.at[:, 0:nf]), (wu, out.at[:, nf : 2 * nf])]
    for i in range(nf // BLK):
        at = 2 * nf + i * BLK
        pairs.append((wd.at[i * BLK : (i + 1) * BLK, :], out.at[:, at : at + BLK]))
    for item in copy_all(pairs, sems):
        item.wait()


def rope(values, cos, sin):
    return values * cos + pltpu.roll(values, HEAD_DIMENSION // 2, 1) * sin


def rope_back(values, cos, sin):
    return values * cos + pltpu.roll(values * sin, HEAD_DIMENSION // 2, 1)


def head(ref, n):
    return ref[:, n * HEAD_DIMENSION : (n + 1) * HEAD_DIMENSION]


def attn_forward(
    ids, x0, x1, x2, x3, q0, q1, q2, q3, cos_r, sin_r, qg_r, kg_r,
    x_out, dy_out, a_out, gains, o_out, qn_out, kn_out, sc_out, qr_out, kr_out, v_out, pr_out,
    t0, t1, t2, t3, qkv, place, sems,
):
    s1 = ids[2]
    qs = (q0, q1, q2, q3)
    nd = qkv.shape[1]
    pairs = [(ref.at[0:BLK, :], x_out.at[s1 ^ SWAP[k]]) for k, ref in enumerate((x0, x1, x2, x3))]
    pairs += [(ref.at[BLK:, :], dy_out.at[s1 ^ SWAP[k]]) for k, ref in enumerate((x0, x1, x2, x3))]
    for item in copy_all(pairs, sems):
        item.wait()
    total = jnp.zeros((BLK, 1), F32)
    for p in range(ROWS):
        x = x_out[p].astype(F32)
        total = total + jnp.sum(x * x, -1, keepdims=True)
        extra = qs[p][BLK : BLK + 16, 0:BLK].astype(F32)
        gains[p : p + 1, :] = extra[0:1] + extra[1:2] + extra[2:3]
        gains[ROWS + p : ROWS + p + 1, :] = extra[3:4] + extra[4:5] + extra[5:6]
    r_one = lax.rsqrt(total / MODEL_WIDTH + epsilon)
    for p in range(ROWS):
        a_out[p] = ((x_out[p].astype(F32) * r_one) * gains[p : p + 1, :]).astype(BF16)
    for p in range(ROWS):
        part = dot(a_out[p], qs[p][0:BLK, 0:nd])
        if p == 0:
            qkv[...] = part
        else:
            qkv[...] += part
    cos, sin = cos_r[...], sin_r[...]
    nkv = kn_out.shape[1] // HEAD_DIMENSION
    nq = qn_out.shape[1] // HEAD_DIMENSION
    lanes = lax.broadcasted_iota(jnp.int32, (BLK, HEAD_DIMENSION), 1)
    packed = jnp.zeros((BLK, HEAD_DIMENSION), F32)
    for n in range(nq + nkv):
        raw = head(qkv, n)
        scale = lax.rsqrt(jnp.mean(raw * raw, -1, keepdims=True) + epsilon)
        packed = jnp.where(lanes == n, scale, packed)
        normed = raw * scale
        cols = slice(n * HEAD_DIMENSION, (n + 1) * HEAD_DIMENSION)
        if n < nq:
            qn_out[:, cols] = normed
            qr_out[:, cols] = rope(normed * qg_r[...], cos, sin).astype(BF16)
        else:
            cols = slice((n - nq) * HEAD_DIMENSION, (n - nq + 1) * HEAD_DIMENSION)
            kn_out[:, cols] = normed
            kr_out[:, cols] = rope(normed * kg_r[...], cos, sin).astype(BF16)
    sc_out[...] = packed
    for n in range(nkv):
        v_out[:, n * HEAD_DIMENSION : (n + 1) * HEAD_DIMENSION] = head(qkv, nq + nkv + n).astype(BF16)
    keep = lax.broadcasted_iota(jnp.int32, (BLK, BLK), 0) >= lax.broadcasted_iota(
        jnp.int32, (BLK, BLK), 1
    )
    factor = HEAD_DIMENSION ** (-0.5)
    for n in range(nq):
        g = n // GROUPS
        scores = jnp.where(keep, dot_nt(head(qr_out, n), head(kr_out, g)) * factor, masked_value)
        top = jnp.max(scores, -1, keepdims=True)
        weights = jnp.exp(scores - top)
        probs = weights / jnp.sum(weights, -1, keepdims=True)
        pr_out[n] = probs
        o_out[:, n * HEAD_DIMENSION : (n + 1) * HEAD_DIMENSION] = dot(
            probs.astype(BF16), head(v_out, g)
        ).astype(BF16)
    for p in range(ROWS):
        acc = dot(o_out[:, 0:BLK], qs[p][0:BLK, nd : nd + BLK])
        for i in range(1, o_out.shape[1] // BLK):
            at = nd + i * BLK
            acc = acc + dot(o_out[:, i * BLK : (i + 1) * BLK], qs[p][0:BLK, at : at + BLK])
        place[p] = acc.astype(BF16)
    for k, slot in enumerate((t0, t1, t2, t3)):
        slot[...] = place[ids[1] ^ k]


def ffn(
    ids, t0, t1, t2, t3, x, dy, f0, f1, f2, f3, gains,
    s0, s1, s2, s3, b_out, m_out, d_out, h_out, gu, da, place,
):
    c = ids[1]
    fs = (f0, f1, f2, f3)
    nf = m_out.shape[1]
    for k, ref in enumerate((t0, t1, t2, t3)):
        h_out[c ^ k] = ref[...].astype(F32)
    total = jnp.zeros((BLK, 1), F32)
    for p in range(ROWS):
        h = h_out[p] + x[p].astype(F32)
        h_out[p] = h
        total = total + jnp.sum(h * h, -1, keepdims=True)
    r_two = lax.rsqrt(total / MODEL_WIDTH + epsilon)
    for p in range(ROWS):
        b_out[p] = ((h_out[p] * r_two) * gains[ROWS + p : ROWS + p + 1, :]).astype(BF16)
    for p in range(ROWS):
        part = dot(b_out[p], fs[p][:, 0 : 2 * nf])
        if p == 0:
            gu[...] = part
        else:
            gu[...] += part
    for i in range(nf // BLK):
        at = slice(2 * nf + i * BLK, 2 * nf + (i + 1) * BLK)
        cols = slice(i * BLK, (i + 1) * BLK)
        acc = dot_nt(dy[0], fs[0][:, at])
        for p in range(1, ROWS):
            acc = acc + dot_nt(dy[p], fs[p][:, at])
        da[:, cols] = acc
    for i in range(nf // BLK):
        cols = slice(i * BLK, (i + 1) * BLK)
        ups = slice(nf + i * BLK, nf + (i + 1) * BLK)
        gate, up, d_act = gu[:, cols], gu[:, ups], da[:, cols]
        sig = 1.0 / (1.0 + jnp.exp(-gate))
        act = gate * sig
        m_out[:, cols] = (act * up).astype(BF16)
        d_out[:, cols] = (d_act * up * sig * (1.0 + gate * (1.0 - sig))).astype(BF16)
        d_out[:, ups] = (d_act * act).astype(BF16)
    for p in range(ROWS):
        place[p] = dot_nt(d_out[...], fs[p][:, 0 : 2 * nf]).astype(BF16)
    for k, slot in enumerate((s0, s1, s2, s3)):
        slot[...] = place[c ^ k]


def down(ids, m, f0, f1, f2, f3, h, place, h_own):
    nf = m.shape[1]
    for p, f in enumerate((f0, f1, f2, f3)):
        acc = jnp.zeros((BLK, BLK), F32)
        for i in range(nf // BLK):
            at = slice(2 * nf + i * BLK, 2 * nf + (i + 1) * BLK)
            acc = acc + dot(m[:, i * BLK : (i + 1) * BLK], f[:, at])
        place[p] = acc.astype(BF16)
    h_own[...] = h[ids[1]]


def ffn_grads(b, d, m, dy, down_s, gu_s, down_k, gu_k):
    nf = m.shape[1]
    for p in range(ROWS):
        out = down_k if p < 2 else down_s
        at = (p % 2) * nf
        out[at : at + nf, :] = dot_tn(m[...], dy[p]).astype(BF16)
    for p in range(ROWS):
        out = gu_k if p < 2 else gu_s
        out[(p % 2) * BLK : (p % 2 + 1) * BLK, :] = dot_tn(b[p], d[...]).astype(BF16)


def proj_grads(o, dh, send, keep):
    width = o.shape[1]
    for p in range(ROWS):
        out = keep if p < 2 else send
        at = (p % 2) * width
        out[at : at + width, :] = dot_tn(o[...], dh[p]).astype(BF16)


def qkv_grads(a, d, send, keep):
    for p in range(ROWS):
        out = keep if p < 2 else send
        out[(p % 2) * BLK : (p % 2 + 1) * BLK, :] = dot_tn(a[p], d[...]).astype(BF16)


def norm_backward(ids, t0, t1, t2, t3, h, dy, gains, w0, w1, w2, w3, dhb, dh_own, d_o, sums, dh):
    r, c = ids[0], ids[1]
    for k, ref in enumerate((t0, t1, t2, t3)):
        dh[c ^ k] = ref[...].astype(F32)
    total = jnp.zeros((BLK, 1), F32)
    for p in range(ROWS):
        total = total + jnp.sum(h[p] * h[p], -1, keepdims=True)
    r_two = lax.rsqrt(total / MODEL_WIDTH + epsilon)
    sums[...] = jnp.zeros(sums.shape, F32)
    first = (c == 0).astype(F32)
    inner = jnp.zeros((BLK, 1), F32)
    for p in range(ROWS):
        n_two = h[p] * r_two
        term = dh[p] * n_two
        sums[pl.ds(ROWS + (r ^ SWAP[p]), 1), :] = jnp.sum(term, 0, keepdims=True) * first
        inner = inner + jnp.sum(term * gains[ROWS + p : ROWS + p + 1, :], -1, keepdims=True)
    inner = inner / MODEL_WIDTH
    for p in range(ROWS):
        n_two = h[p] * r_two
        s_two = dh[p] * gains[ROWS + p : ROWS + p + 1, :]
        out = dy[p].astype(F32) + r_two * (s_two - n_two * inner)
        dh[p] = out
        dhb[p] = out.astype(BF16)
    dh_own[...] = dh[c]
    width = d_o.shape[1]
    for i in range(width // BLK):
        at = slice(w0.shape[1] - width + i * BLK, w0.shape[1] - width + (i + 1) * BLK)
        grad = dot_nt(dhb[0], w0[0:BLK, at])
        for p, w in ((1, w1), (2, w2), (3, w3)):
            grad = grad + dot_nt(dhb[p], w[0:BLK, at])
        d_o[:, i * BLK : (i + 1) * BLK] = grad.astype(BF16)


def attn_backward(
    ids, d_o, sums_in, y_place, gains, x, q0, q1, q2, q3, o, qn, kn, sc, qr, kr, v, pr, cos_r, sin_r, qg_r, kg_r,
    s0, s1, s2, s3, d_qkv, part, sums,
):
    r, c = ids[0], ids[1]
    nq, nkv = qn.shape[1] // HEAD_DIMENSION, kn.shape[1] // HEAD_DIMENSION
    sums[...] = sums_in[...]
    cos, sin = cos_r[...], sin_r[...]
    factor = HEAD_DIMENSION ** (-0.5)
    q_sum = jnp.zeros((1, HEAD_DIMENSION), F32)
    k_sum = jnp.zeros((1, HEAD_DIMENSION), F32)

    def norm_back(grad, normed, scale, gain):
        gained = grad * gain
        return scale * (gained - normed * jnp.mean(gained * normed, -1, keepdims=True))

    for g in range(nkv):
        d_k = jnp.zeros((BLK, HEAD_DIMENSION), F32)
        d_v = jnp.zeros((BLK, HEAD_DIMENSION), F32)
        for n in range(g * GROUPS, (g + 1) * GROUPS):
            grad = head(d_o, n)
            delta = jnp.sum(grad.astype(F32) * head(o, n).astype(F32), -1, keepdims=True)
            probs = pr[n]
            d_v = d_v + dot_tn(probs.astype(BF16), grad)
            d_s = (probs * (dot_nt(grad, head(v, g)) - delta)).astype(BF16)
            d_q = dot(d_s, head(kr, g)) * factor
            d_k = d_k + dot_tn(d_s, head(qr, n))
            e_q = rope_back(d_q, cos, sin)
            normed = head(qn, n)
            q_sum = q_sum + jnp.sum(e_q * normed, 0, keepdims=True)
            d_qkv[:, n * HEAD_DIMENSION : (n + 1) * HEAD_DIMENSION] = norm_back(
                e_q, normed, sc[:, n : n + 1], qg_r[...]
            ).astype(BF16)
        e_k = rope_back(d_k * factor, cos, sin)
        normed = head(kn, g)
        k_sum = k_sum + jnp.sum(e_k * normed, 0, keepdims=True)
        at = (nq + g) * HEAD_DIMENSION
        d_qkv[:, at : at + HEAD_DIMENSION] = norm_back(
            e_k, normed, sc[:, nq + g : nq + g + 1], kg_r[...]
        ).astype(BF16)
        at = (nq + nkv + g) * HEAD_DIMENSION
        d_qkv[:, at : at + HEAD_DIMENSION] = d_v.astype(BF16)
    sums[8:9, 0:HEAD_DIMENSION] = q_sum
    sums[8:9, HEAD_DIMENSION : 2 * HEAD_DIMENSION] = k_sum
    total = jnp.zeros((BLK, 1), F32)
    for p in range(ROWS):
        xf = x[p].astype(F32)
        total = total + jnp.sum(xf * xf, -1, keepdims=True)
    r_one = lax.rsqrt(total / MODEL_WIDTH + epsilon)
    inner = jnp.zeros((BLK, 1), F32)
    for p, q in enumerate((q0, q1, q2, q3)):
        d_a = dot_nt(d_qkv[...], q[0:BLK, 0 : d_qkv.shape[1]])
        term = d_a * (x[p].astype(F32) * r_one)
        sums[pl.ds(r ^ SWAP[p], 1), :] = jnp.sum(term, 0, keepdims=True)
        inner = inner + jnp.sum(term * gains[p : p + 1, :], -1, keepdims=True)
        part[p] = d_a.astype(BF16)
    row = jnp.transpose(jnp.broadcast_to(inner, (BLK, 128)))[0:16, :]
    high = row.astype(BF16).astype(F32)
    ids16 = lax.broadcasted_iota(jnp.int32, (16, BLK), 0)
    tail = jnp.where(ids16 == 0, high, jnp.where(ids16 == 1, row - high, 0.0)).astype(BF16)
    parts = split3(sums[...])
    for k, slot in enumerate((s0, s1, s2, s3)):
        slot[0:BLK, :] = part[c ^ k]
        slot[BLK : 2 * BLK, :] = y_place[c ^ k]
        slot[2 * BLK : 2 * BLK + 16, :] = tail
        for i, item in enumerate(parts):
            slot[2 * BLK + 16 * (i + 1) : 2 * BLK + 16 * (i + 2), :] = item.astype(BF16)


def finish(ids, t0, t1, t2, t3, dh_own, h_own, x, gains, out, sums, each):
    c = ids[1]
    refs = (t0, t1, t2, t3)
    rows = lambda ref, at, n: ref[at : at + n, :].astype(F32)
    d_a = rows(t0, 0, BLK)
    y = h_own[...] + rows(t0, BLK, BLK)
    tail = rows(t0, 2 * BLK, 16)
    for ref in refs[1:]:
        d_a = d_a + rows(ref, 0, BLK)
        y = y + rows(ref, BLK, BLK)
        tail = tail + rows(ref, 2 * BLK, 16)
    for k, ref in enumerate(refs):
        at = 2 * BLK + 16
        each[c ^ k] = rows(ref, at, 16) + rows(ref, at + 16, 16) + rows(ref, at + 32, 16)
    sums[...] = (each[0] + each[1]) + (each[2] + each[3])
    row = jnp.broadcast_to(tail[0:1] + tail[1:2], (128, BLK))
    inner = jnp.transpose(row)[:, 0:1] / MODEL_WIDTH
    total = jnp.zeros((BLK, 1), F32)
    for p in range(ROWS):
        xf = x[p].astype(F32)
        total = total + jnp.sum(xf * xf, -1, keepdims=True)
    r_one = lax.rsqrt(total / MODEL_WIDTH + epsilon)
    gain = gains[pl.ds(c, 1), :]
    n_one = x[c].astype(F32) * r_one
    out[0:BLK, :] = (dh_own[...] + r_one * (d_a * gain - n_one * inner)).astype(BF16)
    out[BLK:, :] = y.astype(BF16)


def row_swap(values, bit):
    return lax.ppermute(values, "row", [(i, i ^ bit) for i in range(ROWS)])


def col_swap(values, bit):
    return lax.ppermute(values, "col", [(i, i ^ bit) for i in range(ROWS)])


def to_sequence(block):
    return [
        lax.ppermute(
            block, ("row", "col"),
            [(r * ROWS + c, c * ROWS + (r ^ k)) for r in range(ROWS) for c in range(ROWS)],
        )
        for k in range(ROWS)
    ]


def to_owner(block):
    return lax.ppermute(
        block, ("row", "col"),
        [(r * ROWS + c, (r ^ SWAP[c]) * ROWS + r) for r in range(ROWS) for c in range(ROWS)],
    )


def after(values, gate):
    return lax.optimization_barrier((values, gate))[0]


def core_stage(send, keep):
    got = row_swap(send, 1)
    half = keep.shape[0] // 2
    mine = keep[:half].astype(F32) + got[:half].astype(F32)
    theirs = keep[half:].astype(F32) + got[half:].astype(F32)
    return mine, theirs.astype(BF16)


def y_stage(parts):
    mine, theirs = parts
    return (mine + row_swap(theirs, 2).astype(F32)).astype(BF16)


def last_sum(own, other, *outs):
    at = 0
    for out in outs:
        cols = slice(at, at + out.shape[1])
        out[...] = own[:, cols].astype(F32) + other[:, cols].astype(F32)
        at = at + out.shape[1]


def last_split(own, total, *outs):
    at = 0
    for out in outs:
        out[...] = total[:, at : at + out.shape[1]]
        at = at + out.shape[1]


def dp_send(n_dp, total):
    if n_dp == 2:
        return lax.ppermute(total, "dp", [(0, 1), (1, 0)])
    return lax.psum(total, "dp").astype(F32)


def scatter_col(slots):
    return [slots[0]] + [col_swap(slots[k], k) for k in range(1, ROWS)]


def gather_col(block):
    return [block] + [col_swap(block, k) for k in range(1, ROWS)]


def add_all(parts):
    total = parts[0].astype(F32)
    for item in parts[1:]:
        total = total + item.astype(F32)
    return total


def per_device(
    n_dp, block_input, query_weight, key_weight, value_weight, projection_weight,
    w_gate, w_up, w_down, attn_gain, ffn_gain, query_gain, key_gain, cotangent,
):
    width_q, width_kv, width_ff = query_weight.shape[1], key_weight.shape[1], w_gate.shape[1]
    width_qkv = width_q + 2 * width_kv
    nq = width_q // HEAD_DIMENSION
    r, c = lax.axis_index("row"), lax.axis_index("col")
    rc = r ^ c
    ids = jnp.stack([r, c, ((rc & 1) << 1) | (rc >> 1)]).astype(jnp.int32)
    cos_np, sin_np = rope_tables()
    cos, sin = jnp.asarray(cos_np), jnp.asarray(sin_np)
    qg, kg = query_gain.reshape(1, -1), key_gain.reshape(1, -1)
    blocks = (ROWS, BLK, BLK)
    slot = sds((BLK, BLK), BF16)

    sem = lambda n: pltpu.SemaphoreType.DMA((n,))
    msg_q, msg_x = call(
        pack_attn, [sds((BLK + 16, width_qkv + width_q), BF16), sds((2 * BLK, BLK), BF16)],
        (query_weight, key_weight, value_weight, projection_weight, block_input, cotangent,
         attn_gain.reshape(1, -1), ffn_gain.reshape(1, -1)),
        [pltpu.VMEM((BLK, BLK), F32), sem(5 + width_q // BLK)], 0, None, (0, 1, 2, 3, 4, 5),
    )
    xs = to_sequence(msg_x)
    q_far = row_swap(msg_q, 2)
    q_all = (msg_q, q_far, row_swap(msg_q, 1), row_swap(q_far, 1))
    (msg_f,) = call(
        pack_ffn, [sds((BLK, 3 * width_ff), BF16)],
        after((w_gate, w_up, w_down), (q_far, xs)), [sem(2 + width_ff // BLK)], 0, None, (0, 1, 2),
    )
    f_far = row_swap(msg_f, 2)

    x_full, dy_full, a_full, gains, o, qn, kn, sc, qr, kr, v, pr, *slots = call(
        attn_forward,
        [
            sds(blocks, BF16), sds(blocks, BF16), sds(blocks, BF16), sds((8, BLK), F32),
            sds((BLK, width_q), BF16),
            sds((BLK, width_q), F32), sds((BLK, width_kv), F32), sds((BLK, HEAD_DIMENSION), F32),
            sds((BLK, width_q), BF16), sds((BLK, width_kv), BF16), sds((BLK, width_kv), BF16),
            sds((nq, BLK, BLK), F32),
        ] + [slot] * ROWS,
        (*xs, *q_all, cos, sin, qg, kg),
        [pltpu.VMEM((BLK, width_qkv), F32), pltpu.VMEM(blocks, BF16), sem(2 * ROWS)],
        2 * BLK * MODEL_WIDTH * (width_qkv + width_q), ids, (0, 1, 2, 3),
    )
    h_slots = scatter_col(slots)
    h_sum = add_all(h_slots).astype(BF16)
    h_parts = gather_col(h_sum)
    f_all = (msg_f, f_far, row_swap(after(msg_f, h_slots), 1), row_swap(after(f_far, h_parts), 1))
    *slots, b_full, m, d_gu, h_full = call(
        ffn,
        [slot] * ROWS
        + [
            sds(blocks, BF16), sds((BLK, width_ff), BF16),
            sds((BLK, 2 * width_ff), BF16), sds(blocks, F32),
        ],
        (*h_parts, x_full, dy_full, *f_all, gains),
        [
            pltpu.VMEM((BLK, 2 * width_ff), F32), pltpu.VMEM((BLK, width_ff), F32),
            pltpu.VMEM(blocks, BF16),
        ],
        10 * BLK * MODEL_WIDTH * width_ff, ids,
    )
    b_slots = scatter_col(slots)
    down_s, gu_s, down_k, gu_k = call(
        ffn_grads, [sds((2 * width_ff, BLK), BF16), sds((2 * BLK, 2 * width_ff), BF16)] * 2,
        (b_full, d_gu, m, dy_full), (), 6 * BLK * MODEL_WIDTH * width_ff,
    )
    mid_down, mid_gu = core_stage(down_s, down_k), core_stage(gu_s, gu_k)
    b_sum = add_all(after(b_slots, (mid_down, mid_gu))).astype(BF16)
    b_parts = gather_col(b_sum)
    y_down, y_gu = y_stage(mid_down), y_stage(mid_gu)
    x_down, x_gu = dp_send(n_dp, y_down), dp_send(n_dp, y_gu)
    y_place, h_own = call(
        down, [sds(blocks, BF16), sds((BLK, BLK), F32)], (m, *f_all, h_full),
        (), 2 * BLK * MODEL_WIDTH * width_ff, ids,
    )

    dh_full, dh_own, d_o, sums = call(
        norm_backward,
        [sds(blocks, BF16), sds((BLK, BLK), F32), sds((BLK, width_q), BF16), sds((16, BLK), F32)],
        (*after(b_parts, (y_down, y_place)), h_full, dy_full, gains, *q_all),
        [pltpu.VMEM(blocks, F32)], 2 * BLK * MODEL_WIDTH * width_q, ids,
    )
    proj_s, proj_k = call(
        proj_grads, [sds((2 * width_q, BLK), BF16)] * 2, (o, dh_full), (),
        2 * BLK * MODEL_WIDTH * width_q,
    )
    *slots, d_qkv = call(
        attn_backward,
        [sds((2 * BLK + 64, BLK), BF16)] * ROWS + [sds((BLK, width_qkv), BF16)],
        (after(d_o, proj_s), sums, y_place, gains, x_full, *q_all,
         o, qn, kn, sc, qr, kr, v, pr, cos, sin, qg, kg),
        [pltpu.VMEM(blocks, BF16), pltpu.VMEM((16, BLK), F32)],
        2 * BLK * MODEL_WIDTH * width_qkv + 10 * BLK * BLK * width_q, ids,
    )
    a_parts = scatter_col(slots)
    qkv_s, qkv_k = call(
        qkv_grads, [sds((2 * BLK, width_qkv), BF16)] * 2,
        (a_full, after(d_qkv, y_gu)), (), 2 * BLK * MODEL_WIDTH * width_qkv,
    )
    mid_proj = core_stage(proj_s, proj_k)
    mid_qkv = core_stage(qkv_s, qkv_k)
    y_proj, y_qkv = y_stage(mid_proj), y_stage(mid_qkv)
    msg_o, sums = call(
        finish, [sds((2 * BLK, BLK), BF16), sds((16, BLK), F32)],
        (*after(a_parts, (y_proj, y_qkv)), dh_own, h_own, x_full, gains),
        [pltpu.VMEM((ROWS, 16, BLK), F32)], 0, ids,
    )
    msg_o = to_owner(msg_o)
    input_grad = msg_o[0:BLK].astype(F32)
    block_output = msg_o[BLK:].astype(F32)
    for bit in (2, 1):
        sums = sums + row_swap(sums, bit)
    other = dp_send(n_dp, sums)
    sums = sums + other if n_dp == 2 else other

    def both(own, other):
        return other if other.dtype == F32 else own.astype(F32) + other.astype(F32)

    y_down, y_gu = after((y_down, y_gu), y_qkv)
    g_down = both(y_down, x_down)
    final = last_sum if n_dp == 2 else last_split
    g_gate, g_up = call(final, [sds((BLK, width_ff), F32)] * 2, (y_gu, x_gu))
    g_proj = both(y_proj, dp_send(n_dp, y_proj))
    g_query, g_key, g_value = call(
        final, [sds((BLK, width_q), F32), sds((BLK, width_kv), F32), sds((BLK, width_kv), F32)],
        (y_qkv, dp_send(n_dp, y_qkv)),
    )
    attn_dgain = lax.dynamic_slice_in_dim(sums, r, 1, 0)[0]
    ffn_dgain = lax.dynamic_slice_in_dim(sums, ROWS + r, 1, 0)[0]
    return (
        block_output,
        input_grad,
        g_query,
        g_key,
        g_value,
        g_proj,
        g_gate,
        g_up,
        g_down,
        attn_dgain,
        ffn_dgain,
        sums[8, :HEAD_DIMENSION],
        sums[8, HEAD_DIMENSION:],
    )


def solution(mesh):
    tokens = P(("dp", "col"), "row")
    return jax.shard_map(
        functools.partial(per_device, mesh.shape["dp"]),
        mesh=mesh,
        in_specs=(
            tokens, P("row", "col"), P("row", "col"), P("row", "col"), P("col", "row"),
            P("row", "col"), P("row", "col"), P("col", "row"), P("row"), P("row"), P(), P(), tokens,
        ),
        out_specs=(
            tokens, tokens, P("row", "col"), P("row", "col"), P("row", "col"), P("col", "row"),
            P("row", "col"), P("row", "col"), P("col", "row"), P("row"), P("row"), P(), P(),
        ),
        check_vma=False,
    )
```

```python
import functools

import jax
import jax.numpy as jnp
import numpy as np
from jax import lax
from jax.experimental import pallas as pl
from jax.experimental.pallas import tpu as pltpu
from jax.sharding import PartitionSpec as P

MODEL_WIDTH = 1024
HEAD_DIMENSION = 128
SEQUENCE_LENGTH = 256
GROUPS = 2

epsilon = 1e-06
rope_base = 1000000.0
masked_value = -1e30

F32 = jnp.float32
BF16 = jnp.bfloat16
BLK = 256
ROWS = 4
SWAP = (0, 2, 1, 3)


def rope_tables():
    places = np.arange(SEQUENCE_LENGTH, dtype=np.float32)
    half = HEAD_DIMENSION // 2
    freqs = np.float32(rope_base) ** (
        -(np.arange(half, dtype=np.float32) * np.float32(2.0)) / np.float32(HEAD_DIMENSION)
    )
    angles = places[:, None] * freqs[None, :].astype(np.float32)
    cos, sin = np.cos(angles), np.sin(angles)
    return np.concatenate([cos, cos, -sin, sin], 1).astype(np.float32)


def dot(left, right):
    return jnp.dot(left, right, preferred_element_type=F32)


def dot_nt(left, right):
    return lax.dot_general(left, right, (((1,), (1,)), ((), ())), preferred_element_type=F32)


def dot_tn(left, right):
    return lax.dot_general(left, right, (((0,), (0,)), ((), ())), preferred_element_type=F32)


def call(body, outs, args, scratch=(), flops=0, smem=None, anywhere=()):
    vm = pl.BlockSpec(memory_space=pltpu.VMEM)
    in_specs = [
        pl.BlockSpec(memory_space=pltpu.HBM) if n in anywhere else vm for n in range(len(args))
    ]
    args = [
        pltpu.with_memory_space_constraint(a, pltpu.HBM) if n in anywhere else a
        for n, a in enumerate(args)
    ]
    if smem is not None:
        in_specs = [pl.BlockSpec(memory_space=pltpu.SMEM)] + in_specs
        args = [smem] + args
    moved = sum(int(np.prod(a.shape)) * a.dtype.itemsize for a in list(args) + list(outs))
    return pl.pallas_call(
        body,
        out_shape=[jax.ShapeDtypeStruct(o.shape, o.dtype) for o in outs],
        in_specs=in_specs,
        out_specs=[vm] * len(outs),
        scratch_shapes=list(scratch),
        compiler_params=pltpu.CompilerParams(vmem_limit_bytes=16 << 20),
        cost_estimate=pl.CostEstimate(flops=flops, bytes_accessed=moved, transcendentals=0),
    )(*args)


def sds(shape, dtype):
    return jax.ShapeDtypeStruct(shape, dtype)


def split3(values):
    high = values.astype(BF16).astype(F32)
    rest = values - high
    mid = rest.astype(BF16).astype(F32)
    return high, mid, rest - mid


def copy_all(pairs, sems):
    copies = [pltpu.make_async_copy(src, dst, sems.at[n]) for n, (src, dst) in enumerate(pairs)]
    for item in copies:
        item.start()
    return copies


def pack_attn(wq, wk, wv, wp, x, dy, ga, gf, out, both, wide, gain, sems):
    nq, nk = wq.shape[1], wk.shape[1]
    pairs = [
        (wq, out.at[0:BLK, 0:nq]),
        (wk, out.at[0:BLK, nq : nq + nk]),
        (wv, out.at[0:BLK, nq + nk : nq + 2 * nk]),
        (x, both.at[0:BLK, :]),
        (dy, wide),
        (ga, gain.at[0:1, :]),
        (gf, gain.at[8:9, :]),
    ]
    for i in range(nq // BLK):
        at = nq + 2 * nk + i * BLK
        pairs.append((wp.at[i * BLK : (i + 1) * BLK, :], out.at[0:BLK, at : at + BLK]))
    copies = copy_all(pairs, sems)
    for item in copies:
        item.wait()
    rows = split3(gain[0:1, :]) + split3(gain[8:9, :])
    ids = lax.broadcasted_iota(jnp.int32, (16, BLK), 0)
    extra = jnp.zeros((16, BLK), F32)
    for n, row in enumerate(rows):
        extra = jnp.where(ids == n, jnp.broadcast_to(row, (16, BLK)), extra)
    out[BLK : BLK + 16, :] = jnp.zeros((16, out.shape[1]), BF16)
    out[BLK : BLK + 16, 0:BLK] = extra.astype(BF16)
    both[BLK:, :] = wide[...].astype(BF16)


def pack_ffn(wg, wu, wd, out, sems):
    nf = wg.shape[1]
    pairs = [(wg, out.at[:, 0:nf]), (wu, out.at[:, nf : 2 * nf])]
    for i in range(nf // BLK):
        at = 2 * nf + i * BLK
        pairs.append((wd.at[i * BLK : (i + 1) * BLK, :], out.at[:, at : at + BLK]))
    for item in copy_all(pairs, sems):
        item.wait()


def rope(values, cos, sin):
    return values * cos + pltpu.roll(values, HEAD_DIMENSION // 2, 1) * sin


def rope_back(values, cos, sin):
    return values * cos + pltpu.roll(values * sin, HEAD_DIMENSION // 2, 1)


def head(ref, n):
    return ref[:, n * HEAD_DIMENSION : (n + 1) * HEAD_DIMENSION]


def attn_forward(
    ids, x0, x1, x2, x3, q0, q1, q2, q3, tables, qg_r, kg_r,
    x_out, dy_out, a_out, gains, o_out, qn_out, kn_out, sc_out, qr_out, kr_out, v_out, pr_out,
    t0, t1, t2, t3, qkv, place, rot, sems,
):
    s1 = ids[2]
    qs = (q0, q1, q2, q3)
    nd = qkv.shape[1]
    pairs = [(ref.at[0:BLK, :], x_out.at[s1 ^ SWAP[k]]) for k, ref in enumerate((x0, x1, x2, x3))]
    pairs += [(ref.at[BLK:, :], dy_out.at[s1 ^ SWAP[k]]) for k, ref in enumerate((x0, x1, x2, x3))]
    pairs.append((tables, rot))
    for item in copy_all(pairs, sems):
        item.wait()
    total = jnp.zeros((BLK, 1), F32)
    for p in range(ROWS):
        x = x_out[p].astype(F32)
        total = total + jnp.sum(x * x, -1, keepdims=True)
        extra = qs[p][BLK : BLK + 16, 0:BLK].astype(F32)
        gains[p : p + 1, :] = extra[0:1] + extra[1:2] + extra[2:3]
        gains[ROWS + p : ROWS + p + 1, :] = extra[3:4] + extra[4:5] + extra[5:6]
    r_one = lax.rsqrt(total / MODEL_WIDTH + epsilon)
    for p in range(ROWS):
        a_out[p] = ((x_out[p].astype(F32) * r_one) * gains[p : p + 1, :]).astype(BF16)
    for p in range(ROWS):
        part = dot(a_out[p], qs[p][0:BLK, 0:nd])
        if p == 0:
            qkv[...] = part
        else:
            qkv[...] += part
    cos, sin = rot[:, :HEAD_DIMENSION], rot[:, HEAD_DIMENSION:]
    nkv = kn_out.shape[1] // HEAD_DIMENSION
    nq = qn_out.shape[1] // HEAD_DIMENSION
    lanes = lax.broadcasted_iota(jnp.int32, (BLK, HEAD_DIMENSION), 1)
    packed = jnp.zeros((BLK, HEAD_DIMENSION), F32)
    for n in range(nq + nkv):
        raw = head(qkv, n)
        scale = lax.rsqrt(jnp.mean(raw * raw, -1, keepdims=True) + epsilon)
        packed = jnp.where(lanes == n, scale, packed)
        normed = raw * scale
        cols = slice(n * HEAD_DIMENSION, (n + 1) * HEAD_DIMENSION)
        if n < nq:
            qn_out[:, cols] = normed
            qr_out[:, cols] = rope(normed * qg_r[...], cos, sin).astype(BF16)
        else:
            cols = slice((n - nq) * HEAD_DIMENSION, (n - nq + 1) * HEAD_DIMENSION)
            kn_out[:, cols] = normed
            kr_out[:, cols] = rope(normed * kg_r[...], cos, sin).astype(BF16)
    sc_out[...] = packed
    for n in range(nkv):
        v_out[:, n * HEAD_DIMENSION : (n + 1) * HEAD_DIMENSION] = head(qkv, nq + nkv + n).astype(BF16)
    keep = lax.broadcasted_iota(jnp.int32, (BLK, BLK), 0) >= lax.broadcasted_iota(
        jnp.int32, (BLK, BLK), 1
    )
    factor = HEAD_DIMENSION ** (-0.5)
    for n in range(nq):
        g = n // GROUPS
        scores = jnp.where(keep, dot_nt(head(qr_out, n), head(kr_out, g)) * factor, masked_value)
        top = jnp.max(scores, -1, keepdims=True)
        weights = jnp.exp(scores - top)
        probs = weights / jnp.sum(weights, -1, keepdims=True)
        pr_out[n] = probs
        o_out[:, n * HEAD_DIMENSION : (n + 1) * HEAD_DIMENSION] = dot(
            probs.astype(BF16), head(v_out, g)
        ).astype(BF16)
    for p in range(ROWS):
        acc = dot(o_out[:, 0:BLK], qs[p][0:BLK, nd : nd + BLK])
        for i in range(1, o_out.shape[1] // BLK):
            at = nd + i * BLK
            acc = acc + dot(o_out[:, i * BLK : (i + 1) * BLK], qs[p][0:BLK, at : at + BLK])
        place[p] = acc.astype(BF16)
    for k, slot in enumerate((t0, t1, t2, t3)):
        slot[...] = place[ids[1] ^ k]


def ffn(
    ids, t0, t1, t2, t3, x, dy, f0, f1, f2, f3, gains,
    s0, s1, s2, s3, b_out, m_out, d_out, h_out, gu, da, place,
):
    c = ids[1]
    fs = (f0, f1, f2, f3)
    nf = m_out.shape[1]
    for k, ref in enumerate((t0, t1, t2, t3)):
        h_out[c ^ k] = ref[...].astype(F32)
    total = jnp.zeros((BLK, 1), F32)
    for p in range(ROWS):
        h = h_out[p] + x[p].astype(F32)
        h_out[p] = h
        total = total + jnp.sum(h * h, -1, keepdims=True)
    r_two = lax.rsqrt(total / MODEL_WIDTH + epsilon)
    for p in range(ROWS):
        b_out[p] = ((h_out[p] * r_two) * gains[ROWS + p : ROWS + p + 1, :]).astype(BF16)
    for p in range(ROWS):
        part = dot(b_out[p], fs[p][:, 0 : 2 * nf])
        if p == 0:
            gu[...] = part
        else:
            gu[...] += part
    for i in range(nf // BLK):
        at = slice(2 * nf + i * BLK, 2 * nf + (i + 1) * BLK)
        cols = slice(i * BLK, (i + 1) * BLK)
        acc = dot_nt(dy[0], fs[0][:, at])
        for p in range(1, ROWS):
            acc = acc + dot_nt(dy[p], fs[p][:, at])
        da[:, cols] = acc
    for i in range(nf // BLK):
        cols = slice(i * BLK, (i + 1) * BLK)
        ups = slice(nf + i * BLK, nf + (i + 1) * BLK)
        gate, up, d_act = gu[:, cols], gu[:, ups], da[:, cols]
        sig = 1.0 / (1.0 + jnp.exp(-gate))
        act = gate * sig
        m_out[:, cols] = (act * up).astype(BF16)
        d_out[:, cols] = (d_act * up * sig * (1.0 + gate * (1.0 - sig))).astype(BF16)
        d_out[:, ups] = (d_act * act).astype(BF16)
    for p in range(ROWS):
        place[p] = dot_nt(d_out[...], fs[p][:, 0 : 2 * nf]).astype(BF16)
    for k, slot in enumerate((s0, s1, s2, s3)):
        slot[...] = place[c ^ k]


def down(ids, m, f0, f1, f2, f3, h, send, keep, h_own, place):
    c = ids[1]
    nf = m.shape[1]
    for p, f in enumerate((f0, f1, f2, f3)):
        acc = jnp.zeros((BLK, BLK), F32)
        for i in range(nf // BLK):
            at = slice(2 * nf + i * BLK, 2 * nf + (i + 1) * BLK)
            acc = acc + dot(m[:, i * BLK : (i + 1) * BLK], f[:, at])
        place[p] = acc.astype(BF16)
    for k, out in enumerate((keep, send)):
        out[0:BLK, :] = place[c ^ k]
        out[BLK:, :] = place[c ^ 2 ^ k]
    h_own[...] = h[c]


def ffn_grads(b, d, m, dy, down_s, gu_s, down_k, gu_k):
    nf = m.shape[1]
    for p in range(ROWS):
        out = down_k if p < 2 else down_s
        at = (p % 2) * nf
        out[at : at + nf, :] = dot_tn(m[...], dy[p]).astype(BF16)
    for p in range(ROWS):
        out = gu_k if p < 2 else gu_s
        out[(p % 2) * BLK : (p % 2 + 1) * BLK, :] = dot_tn(b[p], d[...]).astype(BF16)


def proj_grads(o, dh, send, keep):
    width = o.shape[1]
    for p in range(ROWS):
        out = keep if p < 2 else send
        at = (p % 2) * width
        out[at : at + width, :] = dot_tn(o[...], dh[p]).astype(BF16)


def qkv_grads(a, d, send, keep):
    for p in range(ROWS):
        out = keep if p < 2 else send
        out[(p % 2) * BLK : (p % 2 + 1) * BLK, :] = dot_tn(a[p], d[...]).astype(BF16)


def norm_backward(ids, t0, t1, t2, t3, h, dy, gains, w0, w1, w2, w3, dhb, dh_own, d_o, sums, dh):
    r, c = ids[0], ids[1]
    for k, ref in enumerate((t0, t1, t2, t3)):
        dh[c ^ k] = ref[...].astype(F32)
    total = jnp.zeros((BLK, 1), F32)
    for p in range(ROWS):
        total = total + jnp.sum(h[p] * h[p], -1, keepdims=True)
    r_two = lax.rsqrt(total / MODEL_WIDTH + epsilon)
    sums[...] = jnp.zeros(sums.shape, F32)
    first = (c == 0).astype(F32)
    inner = jnp.zeros((BLK, 1), F32)
    for p in range(ROWS):
        n_two = h[p] * r_two
        term = dh[p] * n_two
        sums[pl.ds(ROWS + (r ^ SWAP[p]), 1), :] = jnp.sum(term, 0, keepdims=True) * first
        inner = inner + jnp.sum(term * gains[ROWS + p : ROWS + p + 1, :], -1, keepdims=True)
    inner = inner / MODEL_WIDTH
    for p in range(ROWS):
        n_two = h[p] * r_two
        s_two = dh[p] * gains[ROWS + p : ROWS + p + 1, :]
        out = dy[p].astype(F32) + r_two * (s_two - n_two * inner)
        dh[p] = out
        dhb[p] = out.astype(BF16)
    dh_own[...] = dh[c]
    width = d_o.shape[1]
    for i in range(width // BLK):
        at = slice(w0.shape[1] - width + i * BLK, w0.shape[1] - width + (i + 1) * BLK)
        grad = dot_nt(dhb[0], w0[0:BLK, at])
        for p, w in ((1, w1), (2, w2), (3, w3)):
            grad = grad + dot_nt(dhb[p], w[0:BLK, at])
        d_o[:, i * BLK : (i + 1) * BLK] = grad.astype(BF16)


def attn_backward(
    ids, d_o, sums_in, gains, x, q0, q1, q2, q3, o, qn, kn, sc, qr, kr, v, pr, tables, qg_r, kg_r,
    msg, sums, d_qkv, rot, sems,
):
    r = ids[0]
    nq, nkv = qn.shape[1] // HEAD_DIMENSION, kn.shape[1] // HEAD_DIMENSION
    (table_copy,) = copy_all([(tables, rot)], sems)
    sums[...] = sums_in[...]
    table_copy.wait()
    cos, sin = rot[:, :HEAD_DIMENSION], rot[:, HEAD_DIMENSION:]
    factor = HEAD_DIMENSION ** (-0.5)
    q_sum = jnp.zeros((1, HEAD_DIMENSION), F32)
    k_sum = jnp.zeros((1, HEAD_DIMENSION), F32)

    def norm_back(grad, normed, scale, gain):
        gained = grad * gain
        return scale * (gained - normed * jnp.mean(gained * normed, -1, keepdims=True))

    for g in range(nkv):
        d_k = jnp.zeros((BLK, HEAD_DIMENSION), F32)
        d_v = jnp.zeros((BLK, HEAD_DIMENSION), F32)
        for n in range(g * GROUPS, (g + 1) * GROUPS):
            grad = head(d_o, n)
            delta = jnp.sum(grad.astype(F32) * head(o, n).astype(F32), -1, keepdims=True)
            probs = pr[n]
            d_v = d_v + dot_tn(probs.astype(BF16), grad)
            d_s = (probs * (dot_nt(grad, head(v, g)) - delta)).astype(BF16)
            d_q = dot(d_s, head(kr, g)) * factor
            d_k = d_k + dot_tn(d_s, head(qr, n))
            e_q = rope_back(d_q, cos, sin)
            normed = head(qn, n)
            q_sum = q_sum + jnp.sum(e_q * normed, 0, keepdims=True)
            d_qkv[:, n * HEAD_DIMENSION : (n + 1) * HEAD_DIMENSION] = norm_back(
                e_q, normed, sc[:, n : n + 1], qg_r[...]
            ).astype(BF16)
        e_k = rope_back(d_k * factor, cos, sin)
        normed = head(kn, g)
        k_sum = k_sum + jnp.sum(e_k * normed, 0, keepdims=True)
        at = (nq + g) * HEAD_DIMENSION
        d_qkv[:, at : at + HEAD_DIMENSION] = norm_back(
            e_k, normed, sc[:, nq + g : nq + g + 1], kg_r[...]
        ).astype(BF16)
        at = (nq + nkv + g) * HEAD_DIMENSION
        d_qkv[:, at : at + HEAD_DIMENSION] = d_v.astype(BF16)
    sums[8:9, 0:HEAD_DIMENSION] = q_sum
    sums[8:9, HEAD_DIMENSION : 2 * HEAD_DIMENSION] = k_sum
    total = jnp.zeros((BLK, 1), F32)
    for p in range(ROWS):
        xf = x[p].astype(F32)
        total = total + jnp.sum(xf * xf, -1, keepdims=True)
    r_one = lax.rsqrt(total / MODEL_WIDTH + epsilon)
    inner = jnp.zeros((BLK, 1), F32)
    for p, q in enumerate((q0, q1, q2, q3)):
        d_a = dot_nt(d_qkv[...], q[0:BLK, 0 : d_qkv.shape[1]])
        term = d_a * (x[p].astype(F32) * r_one)
        sums[pl.ds(r ^ SWAP[p], 1), :] = jnp.sum(term, 0, keepdims=True)
        inner = inner + jnp.sum(term * gains[p : p + 1, :], -1, keepdims=True)
        msg[p, 0:BLK, :] = d_a.astype(BF16)
    row = jnp.transpose(jnp.broadcast_to(inner, (BLK, 128)))[0:16, :]
    high = row.astype(BF16).astype(F32)
    ids16 = lax.broadcasted_iota(jnp.int32, (16, BLK), 0)
    tail = jnp.where(ids16 == 0, high, jnp.where(ids16 == 1, row - high, 0.0)).astype(BF16)
    for p in range(ROWS):
        msg[p, BLK : BLK + 16, :] = tail


def finish(ids, got, dh_own, x, gains, h_own, y_mine, y_got, out):
    c = ids[1]
    rows = lambda at, n: sum(
        (got[p, at : at + n, :].astype(F32) for p in range(1, ROWS)), got[0, at : at + n, :].astype(F32)
    )
    d_a, tail = rows(0, BLK), rows(BLK, 16)
    row = jnp.broadcast_to(tail[0:1] + tail[1:2], (128, BLK))
    inner = jnp.transpose(row)[:, 0:1] / MODEL_WIDTH
    total = jnp.zeros((BLK, 1), F32)
    for p in range(ROWS):
        xf = x[p].astype(F32)
        total = total + jnp.sum(xf * xf, -1, keepdims=True)
    r_one = lax.rsqrt(total / MODEL_WIDTH + epsilon)
    gain = gains[pl.ds(c, 1), :]
    n_one = x[c].astype(F32) * r_one
    out[0:BLK, :] = (dh_own[...] + r_one * (d_a * gain - n_one * inner)).astype(BF16)
    out[BLK:, :] = (h_own[...] + y_mine[...] + y_got[...].astype(F32)).astype(BF16)


def row_swap(values, bit):
    return lax.ppermute(values, "row", [(i, i ^ bit) for i in range(ROWS)])


def col_swap(values, bit):
    return lax.ppermute(values, "col", [(i, i ^ bit) for i in range(ROWS)])


def to_sequence(block):
    return [
        lax.ppermute(
            block, ("row", "col"),
            [(r * ROWS + c, c * ROWS + (r ^ k)) for r in range(ROWS) for c in range(ROWS)],
        )
        for k in range(ROWS)
    ]


def to_owner(block):
    return lax.ppermute(
        block, ("row", "col"),
        [(r * ROWS + c, (r ^ SWAP[c]) * ROWS + r) for r in range(ROWS) for c in range(ROWS)],
    )


def after(values, gate):
    return lax.optimization_barrier((values, gate))[0]


def half_stage(send, keep, swap):
    got = swap(send, 1)
    half = keep.shape[0] // 2
    mine = keep[:half].astype(F32) + got[:half].astype(F32)
    theirs = keep[half:].astype(F32) + got[half:].astype(F32)
    return mine, theirs.astype(BF16)


def core_stage(send, keep):
    return half_stage(send, keep, row_swap)


def y_stage(parts, gate=None):
    mine, theirs = parts
    got = row_swap(theirs, 2)
    if gate is not None:
        got = after(got, gate)
    return (mine + got.astype(F32)).astype(BF16)


def last_sum(own, other, *outs):
    at = 0
    for out in outs:
        cols = slice(at, at + out.shape[1])
        out[...] = own[:, cols].astype(F32) + other[:, cols].astype(F32)
        at = at + out.shape[1]


def last_split(own, total, *outs):
    at = 0
    for out in outs:
        out[...] = total[:, at : at + out.shape[1]]
        at = at + out.shape[1]


def dp_send(n_dp, total):
    if n_dp == 2:
        return lax.ppermute(total, "dp", [(0, 1), (1, 0)])
    return lax.psum(total, "dp").astype(F32)


def both(own, other):
    return other if other.dtype == F32 else own.astype(F32) + other.astype(F32)


def total_sums(n_dp, sums):
    for swap in (row_swap, col_swap):
        for bit in (2, 1):
            sums = sums + swap(sums, bit)
    other = dp_send(n_dp, sums)
    return sums + other if n_dp == 2 else other


def scatter_col(slots):
    return [slots[0]] + [col_swap(slots[k], k) for k in range(1, ROWS)]


def trade_col(blocks):
    return lax.all_to_all(blocks, "col", split_axis=0, concat_axis=0, tiled=True)


def gather_col(block):
    return [block] + [col_swap(block, k) for k in range(1, ROWS)]


def add_all(parts):
    total = parts[0].astype(F32)
    for item in parts[1:]:
        total = total + item.astype(F32)
    return total


def per_device(
    n_dp, block_input, query_weight, key_weight, value_weight, projection_weight,
    w_gate, w_up, w_down, attn_gain, ffn_gain, query_gain, key_gain, cotangent,
):
    width_q, width_kv, width_ff = query_weight.shape[1], key_weight.shape[1], w_gate.shape[1]
    width_qkv = width_q + 2 * width_kv
    nq = width_q // HEAD_DIMENSION
    r, c = lax.axis_index("row"), lax.axis_index("col")
    rc = r ^ c
    ids = jnp.stack([r, c, ((rc & 1) << 1) | (rc >> 1)]).astype(jnp.int32)
    tables = jnp.asarray(rope_tables())
    qg, kg = query_gain.reshape(1, -1), key_gain.reshape(1, -1)
    blocks = (ROWS, BLK, BLK)
    slot = sds((BLK, BLK), BF16)

    sem = lambda n: pltpu.SemaphoreType.DMA((n,))
    msg_q, msg_x = call(
        pack_attn, [sds((BLK + 16, width_qkv + width_q), BF16), sds((2 * BLK, BLK), BF16)],
        (query_weight, key_weight, value_weight, projection_weight, block_input, cotangent,
         attn_gain.reshape(1, -1), ffn_gain.reshape(1, -1)),
        [pltpu.VMEM((BLK, BLK), F32), pltpu.VMEM((16, BLK), F32), sem(7 + width_q // BLK)],
        0, None, range(8),
    )
    xs = to_sequence(msg_x)
    q_far = row_swap(msg_q, 2)
    q_all = (msg_q, q_far, row_swap(msg_q, 1), row_swap(q_far, 1))
    (msg_f,) = call(
        pack_ffn, [sds((BLK, 3 * width_ff), BF16)],
        after((w_gate, w_up, w_down), (q_far, xs)), [sem(2 + width_ff // BLK)], 0, None, (0, 1, 2),
    )
    f_far = row_swap(msg_f, 2)

    x_full, dy_full, a_full, gains, o, qn, kn, sc, qr, kr, v, pr, *slots = call(
        attn_forward,
        [
            sds(blocks, BF16), sds(blocks, BF16), sds(blocks, BF16), sds((8, BLK), F32),
            sds((BLK, width_q), BF16),
            sds((BLK, width_q), F32), sds((BLK, width_kv), F32), sds((BLK, HEAD_DIMENSION), F32),
            sds((BLK, width_q), BF16), sds((BLK, width_kv), BF16), sds((BLK, width_kv), BF16),
            sds((nq, BLK, BLK), F32),
        ] + [slot] * ROWS,
        (*xs, *q_all, tables, qg, kg),
        [pltpu.VMEM((BLK, width_qkv), F32), pltpu.VMEM(blocks, BF16),
         pltpu.VMEM((BLK, 2 * HEAD_DIMENSION), F32), sem(2 * ROWS + 1)],
        2 * BLK * MODEL_WIDTH * (width_qkv + width_q), ids, (0, 1, 2, 3, 8),
    )
    h_slots = scatter_col(slots)
    h_sum = add_all(h_slots).astype(BF16)
    h_parts = gather_col(h_sum)
    f_all = (msg_f, f_far, row_swap(after(msg_f, h_slots), 1), row_swap(after(f_far, h_parts), 1))
    *slots, b_full, m, d_gu, h_full = call(
        ffn,
        [slot] * ROWS
        + [
            sds(blocks, BF16), sds((BLK, width_ff), BF16),
            sds((BLK, 2 * width_ff), BF16), sds(blocks, F32),
        ],
        (*h_parts, x_full, dy_full, *f_all, gains),
        [
            pltpu.VMEM((BLK, 2 * width_ff), F32), pltpu.VMEM((BLK, width_ff), F32),
            pltpu.VMEM(blocks, BF16),
        ],
        10 * BLK * MODEL_WIDTH * width_ff, ids,
    )
    b_slots = scatter_col(slots)
    down_s, gu_s, down_k, gu_k = call(
        ffn_grads, [sds((2 * width_ff, BLK), BF16), sds((2 * BLK, 2 * width_ff), BF16)] * 2,
        (b_full, d_gu, m, dy_full), (), 6 * BLK * MODEL_WIDTH * width_ff,
    )
    mid_down, mid_gu = core_stage(down_s, down_k), core_stage(gu_s, gu_k)
    b_sum = add_all(after(b_slots, (mid_down, mid_gu))).astype(BF16)
    b_parts = gather_col(b_sum)
    y_down, y_gu = y_stage(mid_down), y_stage(mid_gu)
    x_down, x_gu = dp_send(n_dp, y_down), dp_send(n_dp, y_gu)
    y_send, y_keep, h_own = call(
        down, [sds((2 * BLK, BLK), BF16)] * 2 + [sds((BLK, BLK), F32)], (m, *f_all, h_full),
        [pltpu.VMEM(blocks, BF16)], 2 * BLK * MODEL_WIDTH * width_ff, ids,
    )
    y_mine, y_theirs = half_stage(after(y_send, b_parts), y_keep, col_swap)

    dh_full, dh_own, d_o, sums = call(
        norm_backward,
        [sds(blocks, BF16), sds((BLK, BLK), F32), sds((BLK, width_q), BF16), sds((16, BLK), F32)],
        (*after(b_parts, (y_down, y_send)), h_full, dy_full, gains, *q_all),
        [pltpu.VMEM(blocks, F32)], 20 * BLK * MODEL_WIDTH * width_q, ids,
    )
    proj_s, proj_k = call(
        proj_grads, [sds((2 * width_q, BLK), BF16)] * 2, (o, dh_full), (),
        2 * BLK * MODEL_WIDTH * width_q,
    )
    msg_a, sums, d_qkv = call(
        attn_backward,
        [sds((ROWS, BLK + 16, BLK), BF16), sds((16, BLK), F32), sds((BLK, width_qkv), BF16)],
        (after(d_o, proj_s), sums, gains, x_full, *q_all,
         o, qn, kn, sc, qr, kr, v, pr, tables, qg, kg),
        [pltpu.VMEM((BLK, 2 * HEAD_DIMENSION), F32), sem(1)],
        10 * (2 * BLK * MODEL_WIDTH * width_qkv + 10 * BLK * BLK * width_q), ids, (16,),
    )
    mid_proj = core_stage(proj_s, proj_k)
    qkv_s, qkv_k = call(
        qkv_grads, [sds((2 * BLK, width_qkv), BF16)] * 2,
        (a_full, after(d_qkv, (x_down, mid_proj, y_gu))), (),
        40 * BLK * MODEL_WIDTH * width_qkv,
    )
    mid_qkv = core_stage(qkv_s, qkv_k)
    a_parts = trade_col(after(msg_a, mid_qkv))
    y_got = col_swap(y_theirs, 2)
    sums = total_sums(n_dp, after(sums, mid_qkv))
    g_down = both(y_down, x_down)
    y_proj, y_qkv = y_stage(mid_proj), y_stage(mid_qkv, (x_gu, a_parts, y_got, sums, g_down))
    (msg_o,) = call(
        finish, [sds((2 * BLK, BLK), BF16)],
        (after(a_parts, y_qkv), dh_own, x_full, gains, h_own, y_mine, y_got), (), 0, ids,
    )
    msg_o = to_owner(msg_o)
    input_grad = msg_o[0:BLK].astype(F32)
    block_output = msg_o[BLK:].astype(F32)

    y_gu = after(y_gu, y_qkv)
    final = last_sum if n_dp == 2 else last_split
    g_gate, g_up = call(final, [sds((BLK, width_ff), F32)] * 2, (y_gu, x_gu))
    g_proj = both(y_proj, dp_send(n_dp, y_proj))
    g_query, g_key, g_value = call(
        final, [sds((BLK, width_q), F32), sds((BLK, width_kv), F32), sds((BLK, width_kv), F32)],
        (y_qkv, dp_send(n_dp, y_qkv)),
    )
    attn_dgain = lax.dynamic_slice_in_dim(sums, r, 1, 0)[0]
    ffn_dgain = lax.dynamic_slice_in_dim(sums, ROWS + r, 1, 0)[0]
    return (
        block_output,
        input_grad,
        g_query,
        g_key,
        g_value,
        g_proj,
        g_gate,
        g_up,
        g_down,
        attn_dgain,
        ffn_dgain,
        sums[8, :HEAD_DIMENSION],
        sums[8, HEAD_DIMENSION:],
    )


def solution(mesh):
    tokens = P(("dp", "col"), "row")
    return jax.shard_map(
        functools.partial(per_device, mesh.shape["dp"]),
        mesh=mesh,
        in_specs=(
            tokens, P("row", "col"), P("row", "col"), P("row", "col"), P("col", "row"),
            P("row", "col"), P("row", "col"), P("col", "row"), P("row"), P("row"), P(), P(), tokens,
        ),
        out_specs=(
            tokens, tokens, P("row", "col"), P("row", "col"), P("row", "col"), P("col", "row"),
            P("row", "col"), P("row", "col"), P("col", "row"), P("row"), P("row"), P(), P(),
        ),
        check_vma=False,
    )
```

```python
import functools

import jax
import jax.numpy as jnp
import numpy as np
from jax import lax
from jax.experimental import pallas as pl
from jax.experimental.pallas import tpu as pltpu
from jax.sharding import PartitionSpec as P

MODEL_WIDTH = 1024
HEAD_DIMENSION = 128
SEQUENCE_LENGTH = 256
GROUPS = 2

epsilon = 1e-06
rope_base = 1000000.0
masked_value = -1e30

F32 = jnp.float32
BF16 = jnp.bfloat16
BLK = 256
ROWS = 4
SWAP = (0, 2, 1, 3)


def rope_tables():
    places = np.arange(SEQUENCE_LENGTH, dtype=np.float32)
    half = HEAD_DIMENSION // 2
    freqs = np.float32(rope_base) ** (
        -(np.arange(half, dtype=np.float32) * np.float32(2.0)) / np.float32(HEAD_DIMENSION)
    )
    angles = places[:, None] * freqs[None, :].astype(np.float32)
    cos, sin = np.cos(angles), np.sin(angles)
    return np.concatenate([cos, cos, -sin, sin], 1).astype(np.float32)


def dot(left, right):
    return jnp.dot(left, right, preferred_element_type=F32)


def dot_nt(left, right):
    return lax.dot_general(left, right, (((1,), (1,)), ((), ())), preferred_element_type=F32)


def dot_tn(left, right):
    return lax.dot_general(left, right, (((0,), (0,)), ((), ())), preferred_element_type=F32)


def call(body, outs, args, scratch=(), flops=0, smem=None, anywhere=()):
    vm = pl.BlockSpec(memory_space=pltpu.VMEM)
    in_specs = [
        pl.BlockSpec(memory_space=pltpu.HBM) if n in anywhere else vm for n in range(len(args))
    ]
    args = [
        pltpu.with_memory_space_constraint(a, pltpu.HBM) if n in anywhere else a
        for n, a in enumerate(args)
    ]
    if smem is not None:
        in_specs = [pl.BlockSpec(memory_space=pltpu.SMEM)] + in_specs
        args = [smem] + args
    moved = sum(int(np.prod(a.shape)) * a.dtype.itemsize for a in list(args) + list(outs))
    return pl.pallas_call(
        body,
        out_shape=[jax.ShapeDtypeStruct(o.shape, o.dtype) for o in outs],
        in_specs=in_specs,
        out_specs=[vm] * len(outs),
        scratch_shapes=list(scratch),
        compiler_params=pltpu.CompilerParams(vmem_limit_bytes=16 << 20),
        cost_estimate=pl.CostEstimate(flops=flops, bytes_accessed=moved, transcendentals=0),
    )(*args)


def sds(shape, dtype):
    return jax.ShapeDtypeStruct(shape, dtype)


def split3(values):
    high = values.astype(BF16).astype(F32)
    rest = values - high
    mid = rest.astype(BF16).astype(F32)
    return high, mid, rest - mid


def copy_all(pairs, sems):
    copies = [pltpu.make_async_copy(src, dst, sems.at[n]) for n, (src, dst) in enumerate(pairs)]
    for item in copies:
        item.start()
    return copies


def pack_attn(wq, wk, wv, wp, x, dy, ga, gf, out, both, wide, gain, sems):
    nq, nk = wq.shape[1], wk.shape[1]
    pairs = [
        (wq, out.at[0:BLK, 0:nq]),
        (wk, out.at[0:BLK, nq : nq + nk]),
        (wv, out.at[0:BLK, nq + nk : nq + 2 * nk]),
        (x, both.at[0:BLK, :]),
        (dy, wide),
        (ga, gain.at[0:1, :]),
        (gf, gain.at[8:9, :]),
    ]
    for i in range(nq // BLK):
        at = nq + 2 * nk + i * BLK
        pairs.append((wp.at[i * BLK : (i + 1) * BLK, :], out.at[0:BLK, at : at + BLK]))
    copies = copy_all(pairs, sems)
    for item in copies:
        item.wait()
    rows = split3(gain[0:1, :]) + split3(gain[8:9, :])
    ids = lax.broadcasted_iota(jnp.int32, (16, BLK), 0)
    extra = jnp.zeros((16, BLK), F32)
    for n, row in enumerate(rows):
        extra = jnp.where(ids == n, jnp.broadcast_to(row, (16, BLK)), extra)
    out[BLK : BLK + 16, :] = jnp.zeros((16, out.shape[1]), BF16)
    out[BLK : BLK + 16, 0:BLK] = extra.astype(BF16)
    both[BLK:, :] = wide[...].astype(BF16)


def pack_ffn(wg, wu, wd, out, sems):
    nf = wg.shape[1]
    pairs = [(wg, out.at[:, 0:nf]), (wu, out.at[:, nf : 2 * nf])]
    for i in range(nf // BLK):
        at = 2 * nf + i * BLK
        pairs.append((wd.at[i * BLK : (i + 1) * BLK, :], out.at[:, at : at + BLK]))
    for item in copy_all(pairs, sems):
        item.wait()


def rope(values, cos, sin):
    return values * cos + pltpu.roll(values, HEAD_DIMENSION // 2, 1) * sin


def rope_back(values, cos, sin):
    return values * cos + pltpu.roll(values * sin, HEAD_DIMENSION // 2, 1)


def head(ref, n):
    return ref[:, n * HEAD_DIMENSION : (n + 1) * HEAD_DIMENSION]


def attn_forward(
    ids, x0, x1, x2, x3, q0, q1, q2, q3, tables, qg_r, kg_r,
    x_out, dy_out, a_out, gains, o_out, qn_out, kn_out, sc_out, qr_out, kr_out, v_out, pr_out,
    t0, t1, t2, t3, qkv, place, rot, sems,
):
    s1 = ids[2]
    qs = (q0, q1, q2, q3)
    nd = qkv.shape[1]
    pairs = [(ref.at[0:BLK, :], x_out.at[s1 ^ SWAP[k]]) for k, ref in enumerate((x0, x1, x2, x3))]
    pairs += [(ref.at[BLK:, :], dy_out.at[s1 ^ SWAP[k]]) for k, ref in enumerate((x0, x1, x2, x3))]
    pairs.append((tables, rot))
    for item in copy_all(pairs, sems):
        item.wait()
    total = jnp.zeros((BLK, 1), F32)
    for p in range(ROWS):
        x = x_out[p].astype(F32)
        total = total + jnp.sum(x * x, -1, keepdims=True)
        extra = qs[p][BLK : BLK + 16, 0:BLK].astype(F32)
        gains[p : p + 1, :] = extra[0:1] + extra[1:2] + extra[2:3]
        gains[ROWS + p : ROWS + p + 1, :] = extra[3:4] + extra[4:5] + extra[5:6]
    r_one = lax.rsqrt(total / MODEL_WIDTH + epsilon)
    for p in range(ROWS):
        a_out[p] = ((x_out[p].astype(F32) * r_one) * gains[p : p + 1, :]).astype(BF16)
    for p in range(ROWS):
        part = dot(a_out[p], qs[p][0:BLK, 0:nd])
        if p == 0:
            qkv[...] = part
        else:
            qkv[...] += part
    cos, sin = rot[:, :HEAD_DIMENSION], rot[:, HEAD_DIMENSION:]
    nkv = kn_out.shape[1] // HEAD_DIMENSION
    nq = qn_out.shape[1] // HEAD_DIMENSION
    lanes = lax.broadcasted_iota(jnp.int32, (BLK, HEAD_DIMENSION), 1)
    packed = jnp.zeros((BLK, HEAD_DIMENSION), F32)
    for n in range(nq + nkv):
        raw = head(qkv, n)
        scale = lax.rsqrt(jnp.mean(raw * raw, -1, keepdims=True) + epsilon)
        packed = jnp.where(lanes == n, scale, packed)
        normed = raw * scale
        cols = slice(n * HEAD_DIMENSION, (n + 1) * HEAD_DIMENSION)
        if n < nq:
            qn_out[:, cols] = normed
            qr_out[:, cols] = rope(normed * qg_r[...], cos, sin).astype(BF16)
        else:
            cols = slice((n - nq) * HEAD_DIMENSION, (n - nq + 1) * HEAD_DIMENSION)
            kn_out[:, cols] = normed
            kr_out[:, cols] = rope(normed * kg_r[...], cos, sin).astype(BF16)
    sc_out[...] = packed
    for n in range(nkv):
        v_out[:, n * HEAD_DIMENSION : (n + 1) * HEAD_DIMENSION] = head(qkv, nq + nkv + n).astype(BF16)
    keep = lax.broadcasted_iota(jnp.int32, (BLK, BLK), 0) >= lax.broadcasted_iota(
        jnp.int32, (BLK, BLK), 1
    )
    factor = HEAD_DIMENSION ** (-0.5)
    for n in range(nq):
        g = n // GROUPS
        scores = jnp.where(keep, dot_nt(head(qr_out, n), head(kr_out, g)) * factor, masked_value)
        top = jnp.max(scores, -1, keepdims=True)
        weights = jnp.exp(scores - top)
        probs = weights / jnp.sum(weights, -1, keepdims=True)
        pr_out[n] = probs
        o_out[:, n * HEAD_DIMENSION : (n + 1) * HEAD_DIMENSION] = dot(
            probs.astype(BF16), head(v_out, g)
        ).astype(BF16)
    for p in range(ROWS):
        acc = dot(o_out[:, 0:BLK], qs[p][0:BLK, nd : nd + BLK])
        for i in range(1, o_out.shape[1] // BLK):
            at = nd + i * BLK
            acc = acc + dot(o_out[:, i * BLK : (i + 1) * BLK], qs[p][0:BLK, at : at + BLK])
        place[p] = acc.astype(BF16)
    for k, slot in enumerate((t0, t1, t2, t3)):
        slot[...] = place[ids[1] ^ k]


def ffn(
    ids, t0, t1, t2, t3, x, dy, f0, f1, f2, f3, gains,
    s0, s1, s2, s3, b_out, m_out, d_out, h_out, gu, da, place,
):
    c = ids[1]
    fs = (f0, f1, f2, f3)
    nf = m_out.shape[1]
    for k, ref in enumerate((t0, t1, t2, t3)):
        h_out[c ^ k] = ref[...].astype(F32)
    total = jnp.zeros((BLK, 1), F32)
    for p in range(ROWS):
        h = h_out[p] + x[p].astype(F32)
        h_out[p] = h
        total = total + jnp.sum(h * h, -1, keepdims=True)
    r_two = lax.rsqrt(total / MODEL_WIDTH + epsilon)
    for p in range(ROWS):
        b_out[p] = ((h_out[p] * r_two) * gains[ROWS + p : ROWS + p + 1, :]).astype(BF16)
    for p in range(ROWS):
        part = dot(b_out[p], fs[p][:, 0 : 2 * nf])
        if p == 0:
            gu[...] = part
        else:
            gu[...] += part
    for i in range(nf // BLK):
        at = slice(2 * nf + i * BLK, 2 * nf + (i + 1) * BLK)
        cols = slice(i * BLK, (i + 1) * BLK)
        acc = dot_nt(dy[0], fs[0][:, at])
        for p in range(1, ROWS):
            acc = acc + dot_nt(dy[p], fs[p][:, at])
        da[:, cols] = acc
    for i in range(nf // BLK):
        cols = slice(i * BLK, (i + 1) * BLK)
        ups = slice(nf + i * BLK, nf + (i + 1) * BLK)
        gate, up, d_act = gu[:, cols], gu[:, ups], da[:, cols]
        sig = 1.0 / (1.0 + jnp.exp(-gate))
        act = gate * sig
        m_out[:, cols] = (act * up).astype(BF16)
        d_out[:, cols] = (d_act * up * sig * (1.0 + gate * (1.0 - sig))).astype(BF16)
        d_out[:, ups] = (d_act * act).astype(BF16)
    for p in range(ROWS):
        place[p] = dot_nt(d_out[...], fs[p][:, 0 : 2 * nf]).astype(BF16)
    for k, slot in enumerate((s0, s1, s2, s3)):
        slot[...] = place[c ^ k]


def down(ids, m, f0, f1, f2, f3, h, send, keep, h_own, place):
    c = ids[1]
    nf = m.shape[1]
    for p, f in enumerate((f0, f1, f2, f3)):
        acc = jnp.zeros((BLK, BLK), F32)
        for i in range(nf // BLK):
            at = slice(2 * nf + i * BLK, 2 * nf + (i + 1) * BLK)
            acc = acc + dot(m[:, i * BLK : (i + 1) * BLK], f[:, at])
        place[p] = acc.astype(BF16)
    for k, out in enumerate((keep, send)):
        out[0:BLK, :] = place[c ^ k]
        out[BLK:, :] = place[c ^ 2 ^ k]
    h_own[...] = h[c]


def ffn_grads(b, d, m, dy, down_s, gu_s, down_k, gu_k):
    nf = m.shape[1]
    for p in range(ROWS):
        out = down_k if p < 2 else down_s
        at = (p % 2) * nf
        out[at : at + nf, :] = dot_tn(m[...], dy[p]).astype(BF16)
    for p in range(ROWS):
        out = gu_k if p < 2 else gu_s
        out[(p % 2) * BLK : (p % 2 + 1) * BLK, :] = dot_tn(b[p], d[...]).astype(BF16)


def proj_grads(o, dh, send, keep):
    width = o.shape[1]
    for p in range(ROWS):
        out = keep if p < 2 else send
        at = (p % 2) * width
        out[at : at + width, :] = dot_tn(o[...], dh[p]).astype(BF16)


def qkv_grads(a, d, send, keep):
    for p in range(ROWS):
        out = keep if p < 2 else send
        out[(p % 2) * BLK : (p % 2 + 1) * BLK, :] = dot_tn(a[p], d[...]).astype(BF16)


def norm_backward(ids, t0, t1, t2, t3, h, dy, gains, w0, w1, w2, w3, dhb, dh_own, d_o, sums, dh):
    r, c = ids[0], ids[1]
    for k, ref in enumerate((t0, t1, t2, t3)):
        dh[c ^ k] = ref[...].astype(F32)
    total = jnp.zeros((BLK, 1), F32)
    for p in range(ROWS):
        total = total + jnp.sum(h[p] * h[p], -1, keepdims=True)
    r_two = lax.rsqrt(total / MODEL_WIDTH + epsilon)
    sums[...] = jnp.zeros(sums.shape, F32)
    first = (c == 0).astype(F32)
    inner = jnp.zeros((BLK, 1), F32)
    for p in range(ROWS):
        n_two = h[p] * r_two
        term = dh[p] * n_two
        sums[pl.ds(ROWS + (r ^ SWAP[p]), 1), :] = jnp.sum(term, 0, keepdims=True) * first
        inner = inner + jnp.sum(term * gains[ROWS + p : ROWS + p + 1, :], -1, keepdims=True)
    inner = inner / MODEL_WIDTH
    for p in range(ROWS):
        n_two = h[p] * r_two
        s_two = dh[p] * gains[ROWS + p : ROWS + p + 1, :]
        out = dy[p].astype(F32) + r_two * (s_two - n_two * inner)
        dh[p] = out
        dhb[p] = out.astype(BF16)
    dh_own[...] = dh[c]
    width = d_o.shape[1]
    for i in range(width // BLK):
        at = slice(w0.shape[1] - width + i * BLK, w0.shape[1] - width + (i + 1) * BLK)
        grad = dot_nt(dhb[0], w0[0:BLK, at])
        for p, w in ((1, w1), (2, w2), (3, w3)):
            grad = grad + dot_nt(dhb[p], w[0:BLK, at])
        d_o[:, i * BLK : (i + 1) * BLK] = grad.astype(BF16)


def attn_backward(
    ids, d_o, sums_in, gains, x, q0, q1, q2, q3, o, qn, kn, sc, qr, kr, v, pr, tables, qg_r, kg_r,
    msg, sums, d_qkv, rot, sems,
):
    r = ids[0]
    nq, nkv = qn.shape[1] // HEAD_DIMENSION, kn.shape[1] // HEAD_DIMENSION
    (table_copy,) = copy_all([(tables, rot)], sems)
    sums[...] = sums_in[...]
    table_copy.wait()
    cos, sin = rot[:, :HEAD_DIMENSION], rot[:, HEAD_DIMENSION:]
    factor = HEAD_DIMENSION ** (-0.5)
    q_sum = jnp.zeros((1, HEAD_DIMENSION), F32)
    k_sum = jnp.zeros((1, HEAD_DIMENSION), F32)

    def norm_back(grad, normed, scale, gain):
        gained = grad * gain
        return scale * (gained - normed * jnp.mean(gained * normed, -1, keepdims=True))

    for g in range(nkv):
        d_k = jnp.zeros((BLK, HEAD_DIMENSION), F32)
        d_v = jnp.zeros((BLK, HEAD_DIMENSION), F32)
        for n in range(g * GROUPS, (g + 1) * GROUPS):
            grad = head(d_o, n)
            delta = jnp.sum(grad.astype(F32) * head(o, n).astype(F32), -1, keepdims=True)
            probs = pr[n]
            d_v = d_v + dot_tn(probs.astype(BF16), grad)
            d_s = (probs * (dot_nt(grad, head(v, g)) - delta)).astype(BF16)
            d_q = dot(d_s, head(kr, g)) * factor
            d_k = d_k + dot_tn(d_s, head(qr, n))
            e_q = rope_back(d_q, cos, sin)
            normed = head(qn, n)
            q_sum = q_sum + jnp.sum(e_q * normed, 0, keepdims=True)
            d_qkv[:, n * HEAD_DIMENSION : (n + 1) * HEAD_DIMENSION] = norm_back(
                e_q, normed, sc[:, n : n + 1], qg_r[...]
            ).astype(BF16)
        e_k = rope_back(d_k * factor, cos, sin)
        normed = head(kn, g)
        k_sum = k_sum + jnp.sum(e_k * normed, 0, keepdims=True)
        at = (nq + g) * HEAD_DIMENSION
        d_qkv[:, at : at + HEAD_DIMENSION] = norm_back(
            e_k, normed, sc[:, nq + g : nq + g + 1], kg_r[...]
        ).astype(BF16)
        at = (nq + nkv + g) * HEAD_DIMENSION
        d_qkv[:, at : at + HEAD_DIMENSION] = d_v.astype(BF16)
    sums[8:9, 0:HEAD_DIMENSION] = q_sum
    sums[8:9, HEAD_DIMENSION : 2 * HEAD_DIMENSION] = k_sum
    total = jnp.zeros((BLK, 1), F32)
    for p in range(ROWS):
        xf = x[p].astype(F32)
        total = total + jnp.sum(xf * xf, -1, keepdims=True)
    r_one = lax.rsqrt(total / MODEL_WIDTH + epsilon)
    inner = jnp.zeros((BLK, 1), F32)
    for p, q in enumerate((q0, q1, q2, q3)):
        d_a = dot_nt(d_qkv[...], q[0:BLK, 0 : d_qkv.shape[1]])
        term = d_a * (x[p].astype(F32) * r_one)
        sums[pl.ds(r ^ SWAP[p], 1), :] = jnp.sum(term, 0, keepdims=True)
        inner = inner + jnp.sum(term * gains[p : p + 1, :], -1, keepdims=True)
        msg[p, 0:BLK, :] = d_a.astype(BF16)
    row = jnp.transpose(jnp.broadcast_to(inner, (BLK, 128)))[0:16, :]
    high = row.astype(BF16).astype(F32)
    ids16 = lax.broadcasted_iota(jnp.int32, (16, BLK), 0)
    tail = jnp.where(ids16 == 0, high, jnp.where(ids16 == 1, row - high, 0.0)).astype(BF16)
    for p in range(ROWS):
        msg[p, BLK : BLK + 16, :] = tail


def finish(ids, got, dh_own, x, gains, h_own, y_mine, y_got, out):
    c = ids[1]
    rows = lambda at, n: sum(
        (got[p, at : at + n, :].astype(F32) for p in range(1, ROWS)), got[0, at : at + n, :].astype(F32)
    )
    d_a, tail = rows(0, BLK), rows(BLK, 16)
    row = jnp.broadcast_to(tail[0:1] + tail[1:2], (128, BLK))
    inner = jnp.transpose(row)[:, 0:1] / MODEL_WIDTH
    total = jnp.zeros((BLK, 1), F32)
    for p in range(ROWS):
        xf = x[p].astype(F32)
        total = total + jnp.sum(xf * xf, -1, keepdims=True)
    r_one = lax.rsqrt(total / MODEL_WIDTH + epsilon)
    gain = gains[pl.ds(c, 1), :]
    n_one = x[c].astype(F32) * r_one
    out[0:BLK, :] = (dh_own[...] + r_one * (d_a * gain - n_one * inner)).astype(BF16)
    out[BLK:, :] = (h_own[...] + y_mine[...] + y_got[...].astype(F32)).astype(BF16)


def row_swap(values, bit):
    return lax.ppermute(values, "row", [(i, i ^ bit) for i in range(ROWS)])


def col_swap(values, bit):
    return lax.ppermute(values, "col", [(i, i ^ bit) for i in range(ROWS)])


def to_sequence(block):
    return [
        lax.ppermute(
            block, ("row", "col"),
            [(r * ROWS + c, c * ROWS + (r ^ k)) for r in range(ROWS) for c in range(ROWS)],
        )
        for k in range(ROWS)
    ]


def to_owner(block):
    return lax.ppermute(
        block, ("row", "col"),
        [(r * ROWS + c, (r ^ SWAP[c]) * ROWS + r) for r in range(ROWS) for c in range(ROWS)],
    )


def after(values, gate):
    return lax.optimization_barrier((values, gate))[0]


def half_stage(send, keep, swap):
    got = swap(send, 1)
    half = keep.shape[0] // 2
    mine = keep[:half].astype(F32) + got[:half].astype(F32)
    theirs = keep[half:].astype(F32) + got[half:].astype(F32)
    return mine, theirs.astype(BF16)


def core_stage(send, keep):
    return half_stage(send, keep, row_swap)


def y_stage(parts, gate=None):
    mine, theirs = parts
    got = row_swap(theirs, 2)
    if gate is not None:
        got = after(got, gate)
    return (mine + got.astype(F32)).astype(BF16)


def last_sum(own, other, *outs):
    at = 0
    for out in outs:
        cols = slice(at, at + out.shape[1])
        out[...] = own[:, cols].astype(F32) + other[:, cols].astype(F32)
        at = at + out.shape[1]


def last_split(own, total, *outs):
    at = 0
    for out in outs:
        out[...] = total[:, at : at + out.shape[1]]
        at = at + out.shape[1]


def dp_send(n_dp, total):
    if n_dp == 2:
        return lax.ppermute(total, "dp", [(0, 1), (1, 0)])
    return lax.psum(total, "dp").astype(F32)


def both(own, other):
    return other if other.dtype == F32 else own.astype(F32) + other.astype(F32)


def total_sums(n_dp, sums):
    for swap in (row_swap, col_swap):
        for bit in (2, 1):
            sums = sums + swap(sums, bit)
    other = dp_send(n_dp, sums)
    return sums + other if n_dp == 2 else other


def scatter_col(slots):
    return [slots[0]] + [col_swap(slots[k], k) for k in range(1, ROWS)]


def trade_col(blocks):
    return lax.all_to_all(blocks, "col", split_axis=0, concat_axis=0, tiled=True)


def gather_col(block):
    return [block] + [col_swap(block, k) for k in range(1, ROWS)]


def add_all(parts):
    total = parts[0].astype(F32)
    for item in parts[1:]:
        total = total + item.astype(F32)
    return total


def per_device(
    n_dp, block_input, query_weight, key_weight, value_weight, projection_weight,
    w_gate, w_up, w_down, attn_gain, ffn_gain, query_gain, key_gain, cotangent,
):
    width_q, width_kv, width_ff = query_weight.shape[1], key_weight.shape[1], w_gate.shape[1]
    width_qkv = width_q + 2 * width_kv
    nq = width_q // HEAD_DIMENSION
    r, c = lax.axis_index("row"), lax.axis_index("col")
    rc = r ^ c
    ids = jnp.stack([r, c, ((rc & 1) << 1) | (rc >> 1)]).astype(jnp.int32)
    tables = jnp.asarray(rope_tables())
    qg, kg = query_gain.reshape(1, -1), key_gain.reshape(1, -1)
    blocks = (ROWS, BLK, BLK)
    slot = sds((BLK, BLK), BF16)

    sem = lambda n: pltpu.SemaphoreType.DMA((n,))
    msg_q, msg_x = call(
        pack_attn, [sds((BLK + 16, width_qkv + width_q), BF16), sds((2 * BLK, BLK), BF16)],
        (query_weight, key_weight, value_weight, projection_weight, block_input, cotangent,
         attn_gain.reshape(1, -1), ffn_gain.reshape(1, -1)),
        [pltpu.VMEM((BLK, BLK), F32), pltpu.VMEM((16, BLK), F32), sem(7 + width_q // BLK)],
        0, None, range(8),
    )
    xs = to_sequence(msg_x)
    q_far = row_swap(msg_q, 2)
    q_all = (msg_q, q_far, row_swap(msg_q, 1), row_swap(q_far, 1))
    (msg_f,) = call(
        pack_ffn, [sds((BLK, 3 * width_ff), BF16)],
        after((w_gate, w_up, w_down), (q_far, xs)), [sem(2 + width_ff // BLK)], 0, None, (0, 1, 2),
    )
    f_far = row_swap(msg_f, 2)

    x_full, dy_full, a_full, gains, o, qn, kn, sc, qr, kr, v, pr, *slots = call(
        attn_forward,
        [
            sds(blocks, BF16), sds(blocks, BF16), sds(blocks, BF16), sds((8, BLK), F32),
            sds((BLK, width_q), BF16),
            sds((BLK, width_q), F32), sds((BLK, width_kv), F32), sds((BLK, HEAD_DIMENSION), F32),
            sds((BLK, width_q), BF16), sds((BLK, width_kv), BF16), sds((BLK, width_kv), BF16),
            sds((nq, BLK, BLK), F32),
        ] + [slot] * ROWS,
        (*xs, *q_all, tables, qg, kg),
        [pltpu.VMEM((BLK, width_qkv), F32), pltpu.VMEM(blocks, BF16),
         pltpu.VMEM((BLK, 2 * HEAD_DIMENSION), F32), sem(2 * ROWS + 1)],
        2 * BLK * MODEL_WIDTH * (width_qkv + width_q), ids, (0, 1, 2, 3, 8),
    )
    h_slots = scatter_col(slots)
    h_sum = add_all(h_slots).astype(BF16)
    h_parts = gather_col(h_sum)
    f_all = (msg_f, f_far, row_swap(after(msg_f, h_slots), 1), row_swap(after(f_far, h_parts), 1))
    *slots, b_full, m, d_gu, h_full = call(
        ffn,
        [slot] * ROWS
        + [
            sds(blocks, BF16), sds((BLK, width_ff), BF16),
            sds((BLK, 2 * width_ff), BF16), sds(blocks, F32),
        ],
        (*h_parts, x_full, dy_full, *f_all, gains),
        [
            pltpu.VMEM((BLK, 2 * width_ff), F32), pltpu.VMEM((BLK, width_ff), F32),
            pltpu.VMEM(blocks, BF16),
        ],
        10 * BLK * MODEL_WIDTH * width_ff, ids,
    )
    b_slots = scatter_col(slots)
    down_s, gu_s, down_k, gu_k = call(
        ffn_grads, [sds((2 * width_ff, BLK), BF16), sds((2 * BLK, 2 * width_ff), BF16)] * 2,
        (b_full, d_gu, m, dy_full), (), 6 * BLK * MODEL_WIDTH * width_ff,
    )
    mid_down, mid_gu = core_stage(down_s, down_k), core_stage(gu_s, gu_k)
    b_sum = add_all(after(b_slots, (mid_down, mid_gu))).astype(BF16)
    b_parts = gather_col(b_sum)
    y_down, y_gu = y_stage(mid_down), y_stage(mid_gu)
    x_down, x_gu = dp_send(n_dp, y_down), dp_send(n_dp, y_gu)
    y_send, y_keep, h_own = call(
        down, [sds((2 * BLK, BLK), BF16)] * 2 + [sds((BLK, BLK), F32)], (m, *f_all, h_full),
        [pltpu.VMEM(blocks, BF16)], 2 * BLK * MODEL_WIDTH * width_ff, ids,
    )
    y_mine, y_theirs = half_stage(after(y_send, b_parts), y_keep, col_swap)

    dh_full, dh_own, d_o, sums = call(
        norm_backward,
        [sds(blocks, BF16), sds((BLK, BLK), F32), sds((BLK, width_q), BF16), sds((16, BLK), F32)],
        (*after(b_parts, (y_down, y_send)), h_full, dy_full, gains, *q_all),
        [pltpu.VMEM(blocks, F32)], 20 * BLK * MODEL_WIDTH * width_q, ids,
    )
    proj_s, proj_k = call(
        proj_grads, [sds((2 * width_q, BLK), BF16)] * 2, (o, dh_full), (),
        2 * BLK * MODEL_WIDTH * width_q,
    )
    msg_a, sums, d_qkv = call(
        attn_backward,
        [sds((ROWS, BLK + 16, BLK), BF16), sds((16, BLK), F32), sds((BLK, width_qkv), BF16)],
        (after(d_o, proj_s), sums, gains, x_full, *q_all,
         o, qn, kn, sc, qr, kr, v, pr, tables, qg, kg),
        [pltpu.VMEM((BLK, 2 * HEAD_DIMENSION), F32), sem(1)],
        10 * (2 * BLK * MODEL_WIDTH * width_qkv + 10 * BLK * BLK * width_q), ids, (16,),
    )
    mid_proj = core_stage(proj_s, proj_k)
    qkv_s, qkv_k = call(
        qkv_grads, [sds((2 * BLK, width_qkv), BF16)] * 2,
        (a_full, after(d_qkv, (x_down, mid_proj, y_gu))), (),
        2 * BLK * MODEL_WIDTH * width_qkv,
    )
    mid_qkv = core_stage(qkv_s, qkv_k)
    a_parts = trade_col(after(msg_a, qkv_s))
    y_got = col_swap(y_theirs, 2)
    sums = total_sums(n_dp, after(sums, mid_qkv))
    g_down = both(y_down, x_down)
    y_proj, y_qkv = y_stage(mid_proj), y_stage(mid_qkv, (x_gu, a_parts, y_got, sums, g_down))
    (msg_o,) = call(
        finish, [sds((2 * BLK, BLK), BF16)],
        (after(a_parts, y_qkv), dh_own, x_full, gains, h_own, y_mine, y_got), (), 0, ids,
    )
    msg_o = to_owner(msg_o)
    input_grad = msg_o[0:BLK].astype(F32)
    block_output = msg_o[BLK:].astype(F32)

    y_gu = after(y_gu, y_qkv)
    final = last_sum if n_dp == 2 else last_split
    g_gate, g_up = call(final, [sds((BLK, width_ff), F32)] * 2, (y_gu, x_gu))
    g_proj = both(y_proj, dp_send(n_dp, y_proj))
    g_query, g_key, g_value = call(
        final, [sds((BLK, width_q), F32), sds((BLK, width_kv), F32), sds((BLK, width_kv), F32)],
        (y_qkv, dp_send(n_dp, y_qkv)),
    )
    attn_dgain = lax.dynamic_slice_in_dim(sums, r, 1, 0)[0]
    ffn_dgain = lax.dynamic_slice_in_dim(sums, ROWS + r, 1, 0)[0]
    return (
        block_output,
        input_grad,
        g_query,
        g_key,
        g_value,
        g_proj,
        g_gate,
        g_up,
        g_down,
        attn_dgain,
        ffn_dgain,
        sums[8, :HEAD_DIMENSION],
        sums[8, HEAD_DIMENSION:],
    )


def solution(mesh):
    tokens = P(("dp", "col"), "row")
    return jax.shard_map(
        functools.partial(per_device, mesh.shape["dp"]),
        mesh=mesh,
        in_specs=(
            tokens, P("row", "col"), P("row", "col"), P("row", "col"), P("col", "row"),
            P("row", "col"), P("row", "col"), P("col", "row"), P("row"), P("row"), P(), P(), tokens,
        ),
        out_specs=(
            tokens, tokens, P("row", "col"), P("row", "col"), P("row", "col"), P("col", "row"),
            P("row", "col"), P("row", "col"), P("col", "row"), P("row"), P("row"), P(), P(),
        ),
        check_vma=False,
    )
```
